32 devices in a mesh: gx: 8 (over z, x), gy: 4 (over y, core).
Axes of the slice: x: 2, y: 2, z: 4, core: 2. Of those that a mesh axis runs over, the one named last changes fastest.
Arguments:
- features: bfloat16 [20, 32, 32, 1024], P(None, 'gx', 'gy'), may hold values from -6 to 6
- spectral_weight: float32 [2, 16, 16, 20, 20, 128], P(None, None, None, None, None, ('gx', 'gy')), may hold values from -5 to 5
- pointwise_weight: bfloat16 [20, 20], replicated, may hold values from -1.25 to 1.25
- pointwise_bias: float32 [20], replicated, may hold values from -3 to 3
- cotangent: bfloat16 [20, 32, 32, 1024], P(None, 'gx', 'gy'), may hold values from -21 to 21
Outputs:
- layer_output: bfloat16 [20, 32, 32, 1024], P(None, 'gx', 'gy')
- features_gradient: bfloat16 [20, 32, 32, 1024], P(None, 'gx', 'gy')
- spectral_gradient: float32 [2, 16, 16, 20, 20, 128], P(None, None, None, None, None, ('gx', 'gy'))
- pointwise_gradient: float32 [20, 20], replicated
- bias_gradient: float32 [20], replicated
The draws below stay inside these ranges and needn't reach their ends.
All inputs are finite; a program needn't handle non-finite values.
Results may differ from the reference program's by a relative error of at most 0.0065.
Values sent between devices are 32-bit elements; how exact they have to be, the bound alone decides.
No kernel may reach another device: no remote copies, remote signals or barrier semaphores. Data moves between devices by JAX's collectives and lax.ppermute only.
A program may use at most 256 MiB of HBM per device.

```python
import math
import jax
import jax.numpy as jnp
from jax import lax

C = 20
MX = 16
MY = 16
MZ = 16
MT = 8
NZ = 64
NT = 16
CX = 4
NX = 32
NY = 32
ZT = 1024
MZT = 128
CELLS = 1048576
N_GX = 8


def draw_cotangent(key, part):
    noise_key = jax.random.fold_in(jax.random.fold_in(key, 17), 0)
    array_shape = (C, NX, NY, ZT)
    noise_part = jax.random.truncated_normal(noise_key, -4.0, 4.0, array_shape, jnp.float32)
    growth = 1.0 + 2.0 * jnp.arange(NX, dtype=jnp.float32) / (NX - 1)
    return (noise_part * growth[None, :, None, None]).astype(jnp.bfloat16)


def steps_of(stream_key, dims, shards, least, high):
    def one(axis_at, shards_of):
        steps = jax.random.uniform(jax.random.fold_in(jax.random.fold_in(stream_key, 6), axis_at), (shards_of,), jnp.float32, least / len(shards), high / len(shards))
        return jnp.repeat(jnp.exp(steps), dims[axis_at] // shards_of).reshape((-1,) + (1,) * (len(dims) - axis_at - 1))

    level = one(*shards[0])
    for cut in shards[1:]:
        level = level * one(*cut)
    return level


def bell_draw(own_key, extent, deviation, bound, cuts=(), held_as=jnp.bfloat16):
    drawn = deviation * jax.random.normal(own_key, extent, jnp.float32)
    if cuts:
        drawn = drawn * steps_of(own_key, extent, cuts, -0.22, 0.18)
    return jnp.clip(drawn, -bound, bound).astype(held_as)


def setup_inputs(seed: int = 0) -> dict:
    arg_keys = jax.random.split(jax.random.key(seed), 6)
    features = bell_draw(arg_keys[0], (C, NX, NY, ZT), 1.0, 6.0, ((1, 8), (2, 4)))
    spectral_weight = bell_draw(arg_keys[1], (2, MX, MY, C, C, MZT), ((CELLS / (2 * MX * MY * MZT * C)) ** 0.5), 5.0, ((5, 32),), jnp.float32)
    pointwise_weight = bell_draw(arg_keys[2], (C, C), C ** -0.5, 1.25)
    pointwise_bias = bell_draw(arg_keys[3], (C,), 0.5, 3.0, (), jnp.float32)
    cotangent = draw_cotangent(jax.random.fold_in(arg_keys[5], 71), 0)
    return {"features": features, "spectral_weight": spectral_weight, "pointwise_weight": pointwise_weight, "pointwise_bias": pointwise_bias, "cotangent": cotangent}


half_root = 0.7071067811865476
density_norm = 0.3989422804014327
highest = lax.Precision.HIGHEST

def kept_frequencies(length, mode_count):
    column = jnp.arange(mode_count, dtype=jnp.int32)
    return jnp.where(column < mode_count // 2, column, length - mode_count + column)

def complex_table(length, mode_count):
    phases = kept_frequencies(length, mode_count)[:, None] * jnp.arange(length, dtype=jnp.int32)[None, :] % length
    angles = 2.0 * math.pi / length * phases.astype(jnp.float32)
    scaling = 1.0 / math.sqrt(length)
    cosine_part = jnp.cos(angles) * scaling
    sine_part = -jnp.sin(angles) * scaling
    return jnp.stack([jnp.stack([cosine_part, -sine_part]), jnp.stack([sine_part, cosine_part])])

def make_depth_table():
    depth_phase = jnp.arange(NZ, dtype=jnp.int32)[:, None] * kept_frequencies(NZ, MZ)[None, :] % NZ
    time_phase = jnp.arange(NT, dtype=jnp.int32)[:, None] * kept_frequencies(NT, MT)[None, :] % NT
    phases = (depth_phase[:, None, :, None] * NT + time_phase[None, :, None, :] * NZ) % (NZ * NT)
    angles = 2.0 * math.pi / (NZ * NT) * phases.astype(jnp.float32)
    scaling = 1.0 / math.sqrt(NZ * NT)
    entries = jnp.stack([jnp.cos(angles) * scaling, -jnp.sin(angles) * scaling], axis=2)
    return entries.reshape(NZ * NT, 2, MZ * MT).astype(jnp.bfloat16)

def activation(hidden):
    cumulative = 0.5 * (1.0 + lax.erf(hidden * half_root))
    slopes = cumulative + hidden * density_norm * jnp.exp(-0.5 * hidden * hidden)
    return (hidden * cumulative, slopes)

def contract(form, weight_part, value_part):
    return jnp.einsum(form, weight_part, value_part, precision=highest)

def mix_forward(weights, values):
    form = 'abcdm,cabm->dabm'
    real_out = contract(form, weights[0], values[0]) - contract(form, weights[1], values[1])
    imaginary = contract(form, weights[0], values[1]) + contract(form, weights[1], values[0])
    return jnp.stack([real_out, imaginary])

def mix_adjoint(weights, values):
    form = 'abcdm,dabm->cabm'
    real_out = contract(form, weights[0], values[0]) + contract(form, weights[1], values[1])
    imaginary = contract(form, weights[0], values[1]) - contract(form, weights[1], values[0])
    return jnp.stack([real_out, imaginary])

def weight_gradient(back_values, values):
    form = 'dabm,cabm->abcdm'
    real_out = contract(form, back_values[0], values[0]) + contract(form, back_values[1], values[1])
    imaginary = contract(form, back_values[1], values[0]) - contract(form, back_values[0], values[1])
    return jnp.stack([real_out, imaginary])

def reference(features, spectral_weight, pointwise_weight, pointwise_bias, cotangent):
    first_table = complex_table(NX, MX)
    second_table = complex_table(NY, MY)
    depth_rounded = make_depth_table()
    depth_float = lax.optimization_barrier(depth_rounded).astype(jnp.float32)
    weight_float = pointwise_weight.astype(jnp.float32)
    starts = jnp.arange(N_GX, dtype=jnp.int32) * CX

    def take_rows(array, row_start, axis_number):
        return lax.dynamic_slice_in_dim(array, row_start, CX, axis_number)

    def join_rows(stacked):
        return jnp.moveaxis(stacked, 0, 1).reshape(C, NX, NY, NZ * NT)

    def to_depth_modes(cell_data):

        def transform_rows(row_start):
            rows_float = take_rows(cell_data, row_start, 1).astype(jnp.float32)
            return jnp.einsum('cxys,skm->kcxym', rows_float, depth_float, precision=highest)
        stacked = lax.map(transform_rows, starts)
        return jnp.moveaxis(stacked, 0, 2).reshape(2, C, NX, NY, MZ * MT)

    def to_modes(cell_data):
        partly = jnp.einsum('okax,kcxym->ocaym', first_table, cell_data, precision=highest)
        return jnp.einsum('okby,kcaym->ocabm', second_table, partly, precision=highest)

    def to_space(values):
        partly = jnp.einsum('koby,kcabm->ocaym', second_table, values, precision=highest)
        return jnp.einsum('koax,kcaym->ocxym', first_table, partly, precision=highest)
    spectrum = to_modes(to_depth_modes(features))
    mixed_space = to_space(mix_forward(spectral_weight, spectrum))

    def layer_rows(row_start):
        spectral = jnp.einsum('kcxym,skm->cxys', take_rows(mixed_space, row_start, 2), depth_float, precision=highest)
        inputs = take_rows(features, row_start, 1).astype(jnp.float32)
        pointwise = jnp.einsum('ab,axys->bxys', weight_float, inputs, precision=highest)
        hidden = spectral + pointwise + pointwise_bias[:, None, None, None]
        activated, slopes = activation(hidden)
        upstream = take_rows(cotangent, row_start, 1).astype(jnp.float32)
        hidden_gradient = (upstream * slopes).astype(jnp.bfloat16)
        gradient_float = hidden_gradient.astype(jnp.float32)
        weight_terms = jnp.einsum('axys,bxys->ab', inputs, gradient_float, precision=highest)
        bias_terms = lax.optimization_barrier(jnp.sum(gradient_float, axis=(1, 2, 3)))
        return (activated.astype(jnp.bfloat16), hidden_gradient, weight_terms, bias_terms)
    output_rows, gradient_rows, weight_terms, bias_terms = lax.map(layer_rows, starts)
    layer_output = join_rows(output_rows)
    hidden_gradient = join_rows(gradient_rows)
    back_spectrum = to_modes(to_depth_modes(hidden_gradient))
    spectral_gradient = weight_gradient(back_spectrum, spectrum)
    back_space = to_space(mix_adjoint(spectral_weight, back_spectrum))

    def gradient_rows_of(row_start):
        back_cells = jnp.einsum('kcxym,skm->cxys', take_rows(back_space, row_start, 2), depth_float, precision=highest)
        local_float = take_rows(hidden_gradient, row_start, 1).astype(jnp.float32)
        back_pointwise = jnp.einsum('ab,bxys->axys', weight_float, local_float, precision=highest)
        return (back_cells + back_pointwise).astype(jnp.bfloat16)
    features_gradient = join_rows(lax.map(gradient_rows_of, starts))
    scaling = 1.0 / math.sqrt(CELLS)
    pointwise_gradient = lax.optimization_barrier(jnp.sum(weight_terms, axis=0)) * scaling
    bias_gradient = lax.optimization_barrier(jnp.sum(bias_terms, axis=0)) * scaling
    return (layer_output, features_gradient, spectral_gradient, pointwise_gradient, bias_gradient)
```

```python
import functools
import math

import jax
import jax.numpy as jnp
import numpy as np
from jax import lax
from jax.experimental import pallas as pl
from jax.experimental.pallas import tpu as pltpu
from jax.sharding import PartitionSpec as P

C = 20
MX = 16
MY = 16
MZ = 16
MT = 8
NZ = 64
NT = 16
MZT = 128
ZT = NZ * NT
AB = MX * MY
CP = 24
PAIRS = C * 4
BLOCK = 256


half_root = 0.7071067811865476
density_norm = 0.3989422804014327
highest = lax.Precision.HIGHEST
f32 = jnp.float32
bf16 = jnp.bfloat16


def frequencies(length, mode_count):
    column = np.arange(mode_count)
    return np.where(column < mode_count // 2, column, length - mode_count + column)


def depth_rows(devices):
    kz = frequencies(NZ, MZ)
    kt = frequencies(NT, MT)
    z = np.arange(NZ)
    t = np.arange(NT)
    phase = (
        (kz[:, None, None, None] * z[None, None, :, None] * NT)
        + (kt[None, :, None, None] * t[None, None, None, :] * NZ)
    ) % ZT
    angle = 2.0 * np.pi / ZT * phase.reshape(MZT, ZT)
    parts = np.stack([np.cos(angle), -np.sin(angle)]) / math.sqrt(ZT)
    local = MZT // devices
    rows = parts.reshape(2, devices, local, ZT).transpose(1, 0, 2, 3)
    return rows.reshape(2 * MZT, ZT).astype(np.float32)


def plane_table(first_groups, second_groups, first_local, second_local):
    nx = first_groups * first_local
    ny = second_groups * second_local
    kx = frequencies(nx, MX)
    ky = frequencies(ny, MY)
    gx, gy, cx, cy = np.meshgrid(
        np.arange(first_groups),
        np.arange(second_groups),
        np.arange(first_local),
        np.arange(second_local),
        indexing="ij",
    )
    x = (gx * first_local + cx).reshape(-1)
    y = (gy * second_local + cy).reshape(-1)
    ax = 2.0 * np.pi / nx * (kx[:, None] * x[None, :] % nx)
    ay = 2.0 * np.pi / ny * (ky[:, None] * y[None, :] % ny)
    angle = (ax[:, None, :] + ay[None, :, :]).reshape(AB, nx * ny)
    return np.concatenate([np.cos(angle), np.sin(angle)]) / math.sqrt(nx * ny)


def split(values):
    high = values.astype(bf16)
    return high, (values - high.astype(f32)).astype(bf16)


def dot(left, right, dims):
    return lax.dot_general(left, right, (dims, ((), ())), preferred_element_type=f32)


NN = ((1,), (0,))
NT_DIMS = ((1,), (1,))
TN = ((0,), (0,))


def compiler(limit=None):
    return pltpu.CompilerParams(vmem_limit_bytes=limit or 60 * 1024 * 1024)


def whole(memory=pltpu.VMEM):
    return pl.BlockSpec(memory_space=memory)


def depth_kernel(table_ref, cells_ref, out_ref):
    out = dot(table_ref[...], cells_ref[...], NT_DIMS)
    out_ref[...] = out.reshape(out_ref.shape)


def swap_blocks(tiles):
    lane = lax.broadcasted_iota(jnp.int32, tiles[0].shape, tiles[0].ndim - 1)
    axis = tiles[0].ndim - 1
    low = lane < 64
    even = (lane // 32) % 2 == 0
    t0, t1, t2, t3 = tiles

    def far(u, v):
        return jnp.where(low, u, pltpu.roll(v, 64, axis)), jnp.where(low, pltpu.roll(u, 64, axis), v)

    def near(u, v):
        return jnp.where(even, u, pltpu.roll(v, 32, axis)), jnp.where(even, pltpu.roll(u, 96, axis), v)

    a0, a2 = far(t0, t2)
    a1, a3 = far(t1, t3)
    b0, b1 = near(a0, a1)
    b2, b3 = near(a2, a3)
    return b0, b1, b2, b3


def row_sign(shape, top):
    row = lax.broadcasted_iota(jnp.int32, shape, len(shape) - 2)
    return jnp.where(row % 8 < 4, top, -top).astype(f32)


def to_plane_modes(recv_ref, high_ref, low_ref, cells_ref, modes_ref):
    for group in range(C // 4):
        lanes = pl.ds(group * 128, 128)
        tiles = [recv_ref[:, j, :, lanes] for j in range(4)]
        for i, tile in enumerate(swap_blocks(tiles)):
            for s in range(tile.shape[0]):
                cells_ref[pl.ds((group * 4 + i) * 8, 8), pl.ds(s * 128, 128)] = tile[s]
    high, low = split(cells_ref[...])
    out = (
        dot(high, high_ref[...], NT_DIMS)
        + dot(high, low_ref[...], NT_DIMS)
        + dot(low, high_ref[...], NT_DIMS)
    )
    cosine = out[:, :AB].reshape(C, 8, AB)
    sine = out[:, AB:].reshape(C, 8, AB)
    modes_ref[...] = cosine + row_sign(sine.shape, 1.0) * pltpu.roll(sine, 4, 1)


def to_plane_cells(mixed, high_ref, low_ref, cells_ref, out_ref):
    high, low = split(mixed)

    def product(rows):
        return (
            dot(high, high_ref[rows, :], NN)
            + dot(high, low_ref[rows, :], NN)
            + dot(low, high_ref[rows, :], NN)
        ).reshape(C, 8, high_ref.shape[1])

    cosine = product(pl.ds(0, AB))
    sine = product(pl.ds(AB, AB))
    cells_ref[...] = (
        cosine + row_sign(sine.shape, -1.0) * pltpu.roll(sine, 4, 1)
    ).reshape(cells_ref.shape)
    groups = out_ref.shape[0]
    for group in range(C // 4):
        tiles = [
            jnp.stack(
                [
                    cells_ref[pl.ds((group * 4 + i) * 8, 8), pl.ds(s * 128, 128)]
                    for s in range(groups)
                ]
            )
            for i in range(4)
        ]
        for j, tile in enumerate(swap_blocks(tiles)):
            out_ref[:, j, :, pl.ds(group * 128, 128)] = tile


def weight_kernel(weight_ref, out_ref, wide_ref):
    wide_ref[:, pl.ds(0, C)] = weight_ref[0, 0]
    row = lax.broadcasted_iota(jnp.int32, (CP, 128), 0)

    def step(pair, carry):
        rows = wide_ref[pl.ds(pair, 128, stride=PAIRS), :]
        out_ref[0, 0, pair] = jnp.where(row < C, rows.T[:CP], 0.0)
        return carry

    lax.fori_loop(0, PAIRS, step, 0, unroll=4)


def forward_kernel(
    recv_ref, high_ref, low_ref, weight_ref, out_ref, modes_ref, cells_ref, mixed_ref
):
    to_plane_modes(recv_ref, high_ref, low_ref, cells_ref, modes_ref)

    for index in range(8):
        half = index // 4
        mode = index % 4
        lanes = pl.ds(half * 128, 128)
        real = jnp.zeros((CP, 128), f32)
        imag = jnp.zeros((CP, 128), f32)
        for ci in range(C):
            sr = modes_ref[ci, pl.ds(mode, 1), lanes]
            si = modes_ref[ci, pl.ds(mode + 4, 1), lanes]
            wr = weight_ref[0, half, ci * 4 + mode]
            wi = weight_ref[1, half, ci * 4 + mode]
            real = real + (wr * sr - wi * si)
            imag = imag + (wr * si + wi * sr)
        mixed_ref[half, pl.ds(mode, C, stride=8), :] = real[:C]
        mixed_ref[half, pl.ds(mode + 4, C, stride=8), :] = imag[:C]
    mixed = jnp.concatenate([mixed_ref[0], mixed_ref[1]], axis=1)
    to_plane_cells(mixed, high_ref, low_ref, cells_ref, out_ref)


def backward_kernel(
    recv_ref, high_ref, low_ref, weight_ref, sums_ref, out_ref, modes_ref, cells_ref, flat_ref, mixed_ref
):
    to_plane_modes(recv_ref, high_ref, low_ref, cells_ref, modes_ref)
    for half in range(2):
        flat_ref[half, pl.ds(0, C * 8), :] = modes_ref[:, :, pl.ds(half * 128, 128)].reshape(C * 8, 128)
        flat_ref[half, pl.ds(C * 8, (CP - C) * 8), :] = jnp.zeros(((CP - C) * 8, 128), f32)

    for index in range(8):
        half = index // 4
        mode = index % 4
        lanes = pl.ds(half * 128, 128)
        br = flat_ref[half, pl.ds(mode, CP, stride=8), :]
        bi = flat_ref[half, pl.ds(mode + 4, CP, stride=8), :]
        for ci in range(C):
            wr = weight_ref[0, half, ci * 4 + mode]
            wi = weight_ref[1, half, ci * 4 + mode]
            real = jnp.sum(wr * br + wi * bi, axis=0, keepdims=True)
            imag = jnp.sum(wr * bi - wi * br, axis=0, keepdims=True)
            mixed_ref[pl.ds(ci * 8 + mode, 1), lanes] = real
            mixed_ref[pl.ds(ci * 8 + mode + 4, 1), lanes] = imag
    to_plane_cells(mixed_ref[...], high_ref, low_ref, cells_ref, out_ref)
    tail = jnp.broadcast_to(sums_ref[...][None], (out_ref.shape[0], 8, 128))
    for j in range(4):
        out_ref[:, j, :, pl.ds(C * 32, 128)] = tail


def gradient_kernel(forward_ref, backward_ref, out_ref, flat_ref, wide_ref):
    part = pl.program_id(0)
    flat_ref[...] = backward_ref[...].reshape(C * 8, 128)

    for mode in range(4):
        br = flat_ref[pl.ds(mode, C, stride=8), :]
        bi = flat_ref[pl.ds(mode + 4, C, stride=8), :]
        first = jnp.where(part == 0, br, bi)
        second = jnp.where(part == 0, bi, -br)
        for ci in range(C):
            sr = forward_ref[ci, pl.ds(mode, 1), :]
            si = forward_ref[ci, pl.ds(mode + 4, 1), :]
            value = first * sr + second * si
            value = jnp.concatenate([value, jnp.zeros((128 - C, 128), f32)])
            wide_ref[pl.ds(ci * 4 + mode, 128, stride=PAIRS), :] = value.T
    out_ref[0, 0] = wide_ref[:, pl.ds(0, C)]


def activation(hidden):
    cumulative = 0.5 * (1.0 + lax.erf(hidden * half_root))
    slopes = cumulative + hidden * density_norm * jnp.exp(-0.5 * hidden * hidden)
    return (hidden * cumulative, slopes)


def layer_kernel(
    recv_ref, table_ref, cells_ref, mix_ref, bias_ref, cotangent_ref,
    out_ref, gradient_ref, sent_ref, high_ref, low_ref, total_ref,
):
    step = pl.program_id(0)

    @pl.when(step == 0)
    def _():
        high, low = split(recv_ref[...].T)
        high_ref[...] = high
        low_ref[...] = low

    table = table_ref[...]
    hidden = (
        dot(high_ref[...], table, NN)
        + dot(low_ref[...], table, NN)
        + dot(mix_ref[...], cells_ref[...], NN)
        + bias_ref[...]
    )
    activated, slopes = activation(hidden)
    out_ref[...] = activated.astype(bf16)
    gradient = (cotangent_ref[...].astype(f32) * slopes).astype(bf16)
    gradient_ref[...] = gradient
    partial = dot(table, gradient, NT_DIMS)

    @pl.when(step == 0)
    def _():
        total_ref[...] = partial

    @pl.when(step > 0)
    def _():
        total_ref[...] += partial

    @pl.when(step == pl.num_programs(0) - 1)
    def _():
        sent_ref[...] = total_ref[...].reshape(sent_ref.shape)


def sums_kernel(cells_ref, gradient_ref, out_ref):
    rows = C * 32
    gram = dot(cells_ref[...], gradient_ref[...], NT_DIMS)
    row = lax.broadcasted_iota(jnp.int32, (rows, rows), 0)
    column = lax.broadcasted_iota(jnp.int32, (rows, rows), 1)
    kept = jnp.where(row % 32 == column % 32, gram, 0.0)
    folded = jnp.sum(kept.reshape(C, 32, rows), axis=1)
    ones = jnp.ones((8, ZT), bf16)
    bias = dot(ones, gradient_ref[...], NT_DIMS)
    values = jnp.concatenate([folded, bias[:4]], axis=0)
    owner = lax.broadcasted_iota(jnp.int32, (rows, 32), 0) // 32
    slot = lax.broadcasted_iota(jnp.int32, (rows, 32), 1)
    chooser = (owner == slot).astype(f32)
    small = lax.dot_general(
        values, chooser, (NN, ((), ())), precision=highest, preferred_element_type=f32
    )
    out_ref[...] = jnp.concatenate(
        [small[0:8], small[8:16], small[16:24], jnp.zeros((8, 32), f32)], axis=1
    )


def final_kernel(recv_ref, table_ref, gradient_ref, mix_ref, out_ref, sums_ref, high_ref, low_ref):
    step = pl.program_id(0)

    @pl.when(step == 0)
    def _():
        devices = recv_ref.shape[0]
        values = recv_ref[:, :, pl.ds(0, C * 32)].reshape(devices * 8, C * 32)
        high, low = split(values.T)
        high_ref[...] = high
        low_ref[...] = low
        sums_ref[...] = jnp.sum(recv_ref[:, :, pl.ds(C * 32, 128)], axis=0)

    table = table_ref[...]
    out_ref[...] = (
        dot(high_ref[...], table, NN)
        + dot(low_ref[...], table, NN)
        + dot(mix_ref[...], gradient_ref[...], NN)
    ).astype(bf16)


def spread(weight):
    owner = np.arange(C * 32) // 32
    chooser = jnp.asarray((owner[:, None] == np.arange(C)[None, :]).astype(np.float32), bf16)
    wide = dot(dot(chooser, weight, NN).astype(bf16), chooser, NT_DIMS)
    place = jnp.arange(C * 32) % 32
    return jnp.where(place[:, None] == place[None, :], wide, 0.0).astype(bf16)


def exchange(values):
    return lax.all_to_all(values, ("gx", "gy"), split_axis=0, concat_axis=0, tiled=True)


def cost(flops, nbytes):
    return pl.CostEstimate(flops=int(flops), bytes_accessed=int(nbytes), transcendentals=0)


def fast_on_device(features, spectral_weight, pointwise_weight, pointwise_bias, cotangent):
    first_local = features.shape[1]
    second_local = features.shape[2]
    first_groups = lax.axis_size("gx")
    second_groups = lax.axis_size("gy")
    devices = first_groups * second_groups
    local = first_local * second_local
    rows = C * local
    cells = devices * local
    quads = devices // 4
    depth = jnp.asarray(depth_rows(devices)).astype(bf16)
    plane = plane_table(first_groups, second_groups, first_local, second_local)
    plane_high_np = plane.astype(jnp.bfloat16)
    plane_low_np = (plane - plane_high_np.astype(np.float64)).astype(jnp.bfloat16)
    plane_high = jnp.asarray(plane_high_np)
    plane_low = jnp.asarray(plane_low_np)
    flat = features.reshape(rows, ZT)
    sent_shape = jax.ShapeDtypeStruct((devices, 8, rows), f32)
    quad_shape = jax.ShapeDtypeStruct((quads, 4, 8, rows), f32)
    modes_shape = jax.ShapeDtypeStruct((C, 8, AB), f32)

    sent = pl.pallas_call(
        depth_kernel,
        out_shape=sent_shape,
        in_specs=[whole(), whole()],
        out_specs=whole(),
        compiler_params=compiler(),
        name="depth",
    )(depth, flat)
    received = exchange(sent)

    stored = spectral_weight.transpose(0, 1, 2, 3, 5, 4).reshape(2, 2, 128 * PAIRS, C)
    weight = pl.pallas_call(
        weight_kernel,
        out_shape=jax.ShapeDtypeStruct((2, 2, PAIRS, CP, 128), f32),
        grid=(2, 2),
        in_specs=[pl.BlockSpec((1, 1, 128 * PAIRS, C), lambda k, h: (k, h, 0, 0))],
        out_specs=pl.BlockSpec((1, 1, PAIRS, CP, 128), lambda k, h: (k, h, 0, 0, 0)),
        scratch_shapes=[pltpu.VMEM((128 * PAIRS, 128), f32)],
        compiler_params=compiler(),
        cost_estimate=cost(1e6, 25e6),
        name="weights",
    )(stored)
    mix_back = spread(pointwise_weight)
    mix_ahead = spread(pointwise_weight.T)
    bias = jnp.broadcast_to(pointwise_bias[:, None], (C, local)).reshape(rows, 1)

    back_out, modes = pl.pallas_call(
        forward_kernel,
        out_shape=(quad_shape, modes_shape),
        in_specs=[whole()] * 4,
        out_specs=(whole(), whole()),
        scratch_shapes=[pltpu.VMEM((C * 8, cells), f32), pltpu.VMEM((2, C * 8, 128), f32)],
        compiler_params=compiler(),
        name="forward_modes",
    )(received.reshape(quads, 4, 8, rows), plane_high, plane_low, weight)
    returned = exchange(back_out.reshape(devices, 8, rows)).reshape(2 * MZT, rows)

    blocks = ZT // BLOCK
    column = pl.BlockSpec((rows, BLOCK), lambda s: (0, s))
    table_column = pl.BlockSpec((2 * MZT, BLOCK), lambda s: (0, s))
    layer_output, hidden_gradient, sent_back = pl.pallas_call(
        layer_kernel,
        out_shape=(
            jax.ShapeDtypeStruct((rows, ZT), bf16),
            jax.ShapeDtypeStruct((rows, ZT), bf16),
            sent_shape,
        ),
        grid=(blocks,),
        in_specs=[
            pl.BlockSpec((2 * MZT, rows), lambda s: (0, 0)),
            table_column,
            column,
            pl.BlockSpec((rows, rows), lambda s: (0, 0)),
            pl.BlockSpec((rows, 1), lambda s: (0, 0)),
            column,
        ],
        out_specs=(column, column, pl.BlockSpec((devices, 8, rows), lambda s: (0, 0, 0))),
        scratch_shapes=[
            pltpu.VMEM((rows, 2 * MZT), bf16),
            pltpu.VMEM((rows, 2 * MZT), bf16),
            pltpu.VMEM((2 * MZT, rows), f32),
        ],
        compiler_params=compiler(),
        name="layer",
    )(returned, depth, flat, mix_ahead, bias, cotangent.reshape(rows, ZT))
    received_back = exchange(sent_back)

    sums = pl.pallas_call(
        sums_kernel,
        out_shape=jax.ShapeDtypeStruct((8, 128), f32),
        in_specs=[whole()] * 2,
        out_specs=whole(),
        compiler_params=compiler(),
        cost_estimate=cost(1e9, 3e6),
        name="sums",
    )(flat, hidden_gradient)

    wide = rows + 128
    back_cells, back_modes = pl.pallas_call(
        backward_kernel,
        out_shape=(jax.ShapeDtypeStruct((quads, 4, 8, wide), f32), modes_shape),
        in_specs=[whole()] * 5,
        out_specs=(whole(), whole()),
        scratch_shapes=[
            pltpu.VMEM((C * 8, cells), f32),
            pltpu.VMEM((2, CP * 8, 128), f32),
            pltpu.VMEM((C * 8, AB), f32),
        ],
        compiler_params=compiler(),
        name="backward_modes",
    )(received_back.reshape(quads, 4, 8, rows), plane_high, plane_low, weight, sums)
    returned_back = exchange(back_cells.reshape(devices, 8, wide))

    gradient = pl.pallas_call(
        gradient_kernel,
        out_shape=jax.ShapeDtypeStruct((2, 2, 128 * PAIRS, C), f32),
        grid=(2, 2),
        in_specs=[
            pl.BlockSpec((C, 8, 128), lambda k, h: (0, 0, h)),
            pl.BlockSpec((C, 8, 128), lambda k, h: (0, 0, h)),
        ],
        out_specs=pl.BlockSpec((1, 1, 128 * PAIRS, C), lambda k, h: (k, h, 0, 0)),
        scratch_shapes=[pltpu.VMEM((C * 8, 128), f32), pltpu.VMEM((128 * PAIRS, 128), f32)],
        compiler_params=compiler(),
        cost_estimate=cost(1e6, 25e6),
        name="spectral_gradient",
    )(modes, back_modes)
    spectral_gradient = gradient.reshape(2, MX, MY, C, 4, C).transpose(0, 1, 2, 3, 5, 4)

    features_gradient, totals = pl.pallas_call(
        final_kernel,
        out_shape=(jax.ShapeDtypeStruct((rows, ZT), bf16), jax.ShapeDtypeStruct((8, 128), f32)),
        grid=(blocks,),
        in_specs=[
            pl.BlockSpec((devices, 8, wide), lambda s: (0, 0, 0)),
            table_column,
            column,
            pl.BlockSpec((rows, rows), lambda s: (0, 0)),
        ],
        out_specs=(column, pl.BlockSpec((8, 128), lambda s: (0, 0))),
        scratch_shapes=[
            pltpu.VMEM((rows, 2 * MZT), bf16),
            pltpu.VMEM((rows, 2 * MZT), bf16),
        ],
        compiler_params=compiler(),
        name="features_gradient",
    )(returned_back, depth, hidden_gradient, mix_back)

    scaling = 1.0 / math.sqrt(cells * ZT)
    pointwise_gradient = (
        jnp.concatenate([totals[:, 0:C], totals[:, 32 : 32 + C], totals[:4, 64 : 64 + C]]) * scaling
    )
    bias_gradient = totals[4, 64 : 64 + C] * scaling
    return (
        layer_output.reshape(features.shape),
        features_gradient.reshape(features.shape),
        spectral_gradient,
        pointwise_gradient,
        bias_gradient,
    )


def kept_frequencies(length, mode_count):
    column = jnp.arange(mode_count, dtype=jnp.int32)
    return jnp.where(column < mode_count // 2, column, length - mode_count + column)


def complex_table(length, mode_count):
    phases = (
        kept_frequencies(length, mode_count)[:, None]
        * jnp.arange(length, dtype=jnp.int32)[None, :]
        % length
    )
    angles = 2.0 * math.pi / length * phases.astype(jnp.float32)
    scaling = 1.0 / math.sqrt(length)
    cosine_part = jnp.cos(angles) * scaling
    sine_part = -jnp.sin(angles) * scaling
    return jnp.stack([jnp.stack([cosine_part, -sine_part]), jnp.stack([sine_part, cosine_part])])


def make_depth_table():
    depth_phase = jnp.arange(NZ, dtype=jnp.int32)[:, None] * kept_frequencies(NZ, MZ)[None, :] % NZ
    time_phase = jnp.arange(NT, dtype=jnp.int32)[:, None] * kept_frequencies(NT, MT)[None, :] % NT
    phases = (depth_phase[:, None, :, None] * NT + time_phase[None, :, None, :] * NZ) % (NZ * NT)
    angles = 2.0 * math.pi / (NZ * NT) * phases.astype(jnp.float32)
    scaling = 1.0 / math.sqrt(NZ * NT)
    entries = jnp.stack([jnp.cos(angles) * scaling, -jnp.sin(angles) * scaling], axis=2)
    return entries.reshape(NZ * NT, 2, MZ * MT).astype(jnp.bfloat16)


def wide_activation(hidden):
    cumulative = 0.5 * (1.0 + lax.erf(hidden * half_root))
    slopes = cumulative + hidden * density_norm * jnp.exp(-0.5 * hidden * hidden)
    return (hidden * cumulative, slopes)


def contract(form, weight_part, value_part):
    return jnp.einsum(form, weight_part, value_part, precision=highest)


def mix_forward(weights, values):
    form = "abcdm,cabm->dabm"
    real_out = contract(form, weights[0], values[0]) - contract(form, weights[1], values[1])
    imaginary = contract(form, weights[0], values[1]) + contract(form, weights[1], values[0])
    return jnp.stack([real_out, imaginary])


def mix_adjoint(weights, values):
    form = "abcdm,dabm->cabm"
    real_out = contract(form, weights[0], values[0]) + contract(form, weights[1], values[1])
    imaginary = contract(form, weights[0], values[1]) - contract(form, weights[1], values[0])
    return jnp.stack([real_out, imaginary])


def weight_gradient(back_values, values):
    form = "dabm,cabm->abcdm"
    real_out = contract(form, back_values[0], values[0]) + contract(form, back_values[1], values[1])
    imaginary = contract(form, back_values[1], values[0]) - contract(
        form, back_values[0], values[1]
    )
    return jnp.stack([real_out, imaginary])


def on_device(features, spectral_weight, pointwise_weight, pointwise_bias, cotangent):
    first_local = features.shape[1]
    second_local = features.shape[2]
    first_groups = lax.axis_size("gx")
    second_groups = lax.axis_size("gy")
    first_table = complex_table(first_local * first_groups, MX)
    second_table = complex_table(second_local * second_groups, MY)
    depth_rounded = make_depth_table()
    depth_float = lax.optimization_barrier(depth_rounded).astype(jnp.float32)
    first_grid_table = first_table.reshape(2, 2, MX, first_groups, first_local)
    second_grid_table = second_table.reshape(2, 2, MY, second_groups, second_local)

    def to_modes(cell_data):
        flattened = cell_data.reshape(2, C, first_local * second_local, MZT)
        arrived = lax.all_to_all(flattened, ("gx", "gy"), split_axis=3, concat_axis=2, tiled=True)
        blocks_grid = arrived.reshape(
            2, C, first_groups, second_groups, first_local, second_local, arrived.shape[3]
        )
        partly = jnp.einsum(
            "okagx,kcghxym->ocahym", first_grid_table, blocks_grid, precision=highest
        )
        return jnp.einsum("okbhy,kcahym->ocabm", second_grid_table, partly, precision=highest)

    def to_cells(values):
        partly = jnp.einsum("kobhy,kcabm->ocahym", second_grid_table, values, precision=highest)
        blocks_grid = jnp.einsum(
            "koagx,kcahym->ocghxym", first_grid_table, partly, precision=highest
        )
        flattened = blocks_grid.reshape(
            2, C, first_groups * second_groups * first_local * second_local, blocks_grid.shape[6]
        )
        returned = lax.all_to_all(flattened, ("gx", "gy"), split_axis=2, concat_axis=3, tiled=True)
        return returned.reshape(2, C, first_local, second_local, MZT)

    spectrum_cells = jnp.einsum(
        "cxys,skm->kcxym", features, depth_rounded, preferred_element_type=jnp.float32
    )
    spectrum = to_modes(spectrum_cells)
    mixed_modes = mix_forward(spectral_weight, spectrum)
    spectral = jnp.einsum("kcxym,skm->cxys", to_cells(mixed_modes), depth_float, precision=highest)
    pointwise = jnp.einsum(
        "ab,axys->bxys", pointwise_weight, features, preferred_element_type=jnp.float32
    )
    hidden = spectral + pointwise + pointwise_bias[:, None, None, None]
    activated, slopes = wide_activation(hidden)
    layer_output = activated.astype(jnp.bfloat16)
    hidden_gradient = (cotangent.astype(jnp.float32) * slopes).astype(jnp.bfloat16)
    weight_terms = jnp.einsum(
        "axys,bxys->ab", features, hidden_gradient, preferred_element_type=jnp.float32
    )
    bias_terms = jnp.sum(hidden_gradient, axis=(1, 2, 3), dtype=jnp.float32)
    weight_total, bias_total = lax.psum((weight_terms, bias_terms), ("gx", "gy"))
    back_input = jnp.einsum(
        "cxys,skm->kcxym", hidden_gradient, depth_rounded, preferred_element_type=jnp.float32
    )
    back_spectrum = to_modes(back_input)
    spectral_gradient = weight_gradient(back_spectrum, spectrum)
    back_mixed = mix_adjoint(spectral_weight, back_spectrum)
    back_cells = jnp.einsum("kcxym,skm->cxys", to_cells(back_mixed), depth_float, precision=highest)
    back_pointwise = jnp.einsum(
        "ab,bxys->axys", pointwise_weight, hidden_gradient, preferred_element_type=jnp.float32
    )
    features_gradient = (back_cells + back_pointwise).astype(jnp.bfloat16)
    total_cells = first_local * first_groups * second_local * second_groups * NZ * NT
    scaling = 1.0 / math.sqrt(total_cells)
    return (
        layer_output,
        features_gradient,
        spectral_gradient,
        weight_total * scaling,
        bias_total * scaling,
    )


def place(features, spectral_weight, pointwise_weight, pointwise_bias, cotangent):
    fits = (
        spectral_weight.shape[5] == 4
        and features.shape[1] * features.shape[2] == 32
        and features.shape[3] == ZT
    )
    run = fast_on_device if fits else on_device
    return run(features, spectral_weight, pointwise_weight, pointwise_bias, cotangent)


def solution(mesh):
    return jax.shard_map(
        place,
        mesh=mesh,
        in_specs=(
            P(None, "gx", "gy", None),
            P(None, None, None, None, None, ("gx", "gy")),
            P(),
            P(),
            P(None, "gx", "gy", None),
        ),
        out_specs=(
            P(None, "gx", "gy", None),
            P(None, "gx", "gy", None),
            P(None, None, None, None, None, ("gx", "gy")),
            P(),
            P(),
        ),
        check_vma=False,
    )
```

```python
import functools
import math

import jax
import jax.numpy as jnp
import numpy as np
from jax import lax
from jax.experimental import pallas as pl
from jax.experimental.pallas import tpu as pltpu
from jax.sharding import PartitionSpec as P

C = 20
MX = 16
MY = 16
MZ = 16
MT = 8
NZ = 64
NT = 16
MZT = 128
ZT = NZ * NT
AB = MX * MY
CP = 24
PAIRS = C * 4
BLOCK = 256


half_root = 0.7071067811865476
density_norm = 0.3989422804014327
highest = lax.Precision.HIGHEST
f32 = jnp.float32
bf16 = jnp.bfloat16


def frequencies(length, mode_count):
    column = np.arange(mode_count)
    return np.where(column < mode_count // 2, column, length - mode_count + column)


def depth_rows(devices):
    kz = frequencies(NZ, MZ)
    kt = frequencies(NT, MT)
    z = np.arange(NZ)
    t = np.arange(NT)
    phase = (
        (kz[:, None, None, None] * z[None, None, :, None] * NT)
        + (kt[None, :, None, None] * t[None, None, None, :] * NZ)
    ) % ZT
    angle = 2.0 * np.pi / ZT * phase.reshape(MZT, ZT)
    parts = np.stack([np.cos(angle), -np.sin(angle)]) / math.sqrt(ZT)
    local = MZT // devices
    rows = parts.reshape(2, devices, local, ZT).transpose(1, 0, 2, 3)
    return rows.reshape(2 * MZT, ZT).astype(np.float32)


def split(values):
    high = values.astype(bf16)
    return high, (values - high.astype(f32)).astype(bf16)


def dot(left, right, dims):
    return lax.dot_general(left, right, (dims, ((), ())), preferred_element_type=f32)


NN = ((1,), (0,))
NT_DIMS = ((1,), (1,))
TN = ((0,), (0,))


def start(source, target, sem):
    copy = pltpu.make_async_copy(source, target, sem)
    copy.start()
    return copy


def compiler(mebibytes):
    return pltpu.CompilerParams(vmem_limit_bytes=mebibytes * 1024 * 1024)


def whole(memory=pltpu.VMEM):
    return pl.BlockSpec(memory_space=memory)


def in_hbm(shape, dtype):
    return pltpu.HBM(shape, dtype)


def from_hbm(values):
    return pltpu.with_memory_space_constraint(values, pltpu.HBM)


def depth_kernel(table_hbm, cells_hbm, out_hbm, table_ref, cells_ref, out_ref, sems):
    table_copy = start(table_hbm, table_ref, sems.at[0])
    groups = cells_ref.shape[0] // 128
    blocks = [pl.ds(g * 128, 128) for g in range(groups)]
    arriving = [
        start(cells_hbm.at[block], cells_ref.at[block], sems.at[1 + g])
        for g, block in enumerate(blocks)
    ]
    table_copy.wait()
    leaving = []
    for g, block in enumerate(blocks):
        arriving[g].wait()
        out = dot(table_ref[...], cells_ref[block, :], NT_DIMS)
        out_ref[:, :, block] = out.reshape(out_ref.shape[0], 8, 128)
        leaving.append(
            start(out_ref.at[:, :, block], out_hbm.at[:, :, block], sems.at[1 + groups + g])
        )
    for copy in leaving:
        copy.wait()


def swap_blocks(tiles):
    lane = lax.broadcasted_iota(jnp.int32, tiles[0].shape, tiles[0].ndim - 1)
    axis = tiles[0].ndim - 1
    low = lane < 64
    even = (lane // 32) % 2 == 0
    t0, t1, t2, t3 = tiles

    def far(u, v):
        return jnp.where(low, u, pltpu.roll(v, 64, axis)), jnp.where(low, pltpu.roll(u, 64, axis), v)

    def near(u, v):
        return jnp.where(even, u, pltpu.roll(v, 32, axis)), jnp.where(even, pltpu.roll(u, 96, axis), v)

    a0, a2 = far(t0, t2)
    a1, a3 = far(t1, t3)
    b0, b1 = near(a0, a1)
    b2, b3 = near(a2, a3)
    return b0, b1, b2, b3


def row_sign(shape, top):
    row = lax.broadcasted_iota(jnp.int32, shape, len(shape) - 2)
    return jnp.where(row % 8 < 4, top, -top).astype(f32)


def to_plane_modes(recv_ref, high_ref, low_ref, cells_ref, modes_ref):
    for group in range(C // 4):
        lanes = pl.ds(group * 128, 128)
        tiles = [recv_ref[:, j, :, lanes] for j in range(4)]
        for i, tile in enumerate(swap_blocks(tiles)):
            for s in range(tile.shape[0]):
                cells_ref[pl.ds((group * 4 + i) * 8, 8), pl.ds(s * 128, 128)] = tile[s]
    high, low = split(cells_ref[...])
    out = (
        dot(high, high_ref[...], NT_DIMS)
        + dot(high, low_ref[...], NT_DIMS)
        + dot(low, high_ref[...], NT_DIMS)
    )
    cosine = out[:, :AB].reshape(C, 8, AB)
    sine = out[:, AB:].reshape(C, 8, AB)
    modes_ref[...] = cosine + row_sign(sine.shape, 1.0) * pltpu.roll(sine, 4, 1)


def to_plane_cells(mixed, high_ref, low_ref, cells_ref, out_ref, out_hbm, sems):
    high, low = split(mixed)

    def product(rows):
        return (
            dot(high, high_ref[rows, :], NN)
            + dot(high, low_ref[rows, :], NN)
            + dot(low, high_ref[rows, :], NN)
        ).reshape(C, 8, high_ref.shape[1])

    cosine = product(pl.ds(0, AB))
    sine = product(pl.ds(AB, AB))
    cells_ref[...] = (
        cosine + row_sign(sine.shape, -1.0) * pltpu.roll(sine, 4, 1)
    ).reshape(cells_ref.shape)
    groups = out_ref.shape[0]
    copies = []
    for group in range(C // 4):
        tiles = [
            jnp.stack(
                [
                    cells_ref[pl.ds((group * 4 + i) * 8, 8), pl.ds(s * 128, 128)]
                    for s in range(groups)
                ]
            )
            for i in range(4)
        ]
        lanes = pl.ds(group * 128, 128)
        for j, tile in enumerate(swap_blocks(tiles)):
            out_ref[:, j, :, lanes] = tile
        copies.append(
            start(out_ref.at[:, :, :, lanes], out_hbm.at[:, :, :, lanes], sems.at[group])
        )
    return copies


def weight_kernel(weight_ref, out_ref, wide_ref):
    wide_ref[:, pl.ds(0, C)] = weight_ref[0, 0]
    row = lax.broadcasted_iota(jnp.int32, (CP, 128), 0)

    def step(pair, carry):
        rows = wide_ref[pl.ds(pair, 128, stride=PAIRS), :]
        out_ref[0, pair % 4, 0, pair // 4] = jnp.where(row < C, rows.T[:CP], 0.0)
        return carry

    lax.fori_loop(0, PAIRS, step, 0, unroll=4)


def fetch_weights(weight_hbm, weight_ref, sems):
    return [
        start(
            weight_hbm.at[index // 4, index % 4], weight_ref.at[index // 4, index % 4], sems.at[13 + index]
        )
        for index in range(8)
    ]


def forward_kernel(
    recv_ref, high_ref, low_ref, weight_hbm, out_hbm, modes_out,
    weight_ref, modes_ref, cells_ref, mixed_ref, out_ref, sems,
):
    weights = fetch_weights(weight_hbm, weight_ref, sems)
    to_plane_modes(recv_ref, high_ref, low_ref, cells_ref, modes_ref)
    copies = [start(modes_ref, modes_out, sems.at[11])]

    for index in range(8):
        half = index // 4
        mode = index % 4
        lanes = pl.ds(half * 128, 128)
        weights[index].wait()
        real = jnp.zeros((CP, 128), f32)
        imag = jnp.zeros((CP, 128), f32)
        for ci in range(C):
            sr = modes_ref[ci, pl.ds(mode, 1), lanes]
            si = modes_ref[ci, pl.ds(mode + 4, 1), lanes]
            wr = weight_ref[half, mode, 0, ci]
            wi = weight_ref[half, mode, 1, ci]
            real = real + (wr * sr - wi * si)
            imag = imag + (wr * si + wi * sr)
        mixed_ref[half, pl.ds(mode, C, stride=8), :] = real[:C]
        mixed_ref[half, pl.ds(mode + 4, C, stride=8), :] = imag[:C]
    mixed = jnp.concatenate([mixed_ref[0], mixed_ref[1]], axis=1)
    copies += to_plane_cells(mixed, high_ref, low_ref, cells_ref, out_ref, out_hbm, sems)
    for copy in copies:
        copy.wait()


def backward_kernel(
    recv_ref, high_ref, low_ref, weight_hbm, sums_ref, out_hbm, modes_out,
    weight_ref, modes_ref, cells_ref, flat_ref, mixed_ref, out_ref, sems,
):
    weights = fetch_weights(weight_hbm, weight_ref, sems)
    tail = jnp.broadcast_to(sums_ref[...][None], (out_ref.shape[0], 8, 128))
    lanes = pl.ds(C * 32, 128)
    for j in range(4):
        out_ref[:, j, :, lanes] = tail
    copies = [start(out_ref.at[:, :, :, lanes], out_hbm.at[:, :, :, lanes], sems.at[12])]
    to_plane_modes(recv_ref, high_ref, low_ref, cells_ref, modes_ref)
    copies.append(start(modes_ref, modes_out, sems.at[11]))
    for half in range(2):
        flat_ref[half, pl.ds(0, C * 8), :] = modes_ref[:, :, pl.ds(half * 128, 128)].reshape(C * 8, 128)
        flat_ref[half, pl.ds(C * 8, (CP - C) * 8), :] = jnp.zeros(((CP - C) * 8, 128), f32)

    for index in range(8):
        half = index // 4
        mode = index % 4
        lanes = pl.ds(half * 128, 128)
        weights[index].wait()
        br = flat_ref[half, pl.ds(mode, CP, stride=8), :]
        bi = flat_ref[half, pl.ds(mode + 4, CP, stride=8), :]
        for ci in range(C):
            wr = weight_ref[half, mode, 0, ci]
            wi = weight_ref[half, mode, 1, ci]
            real = jnp.sum(wr * br + wi * bi, axis=0, keepdims=True)
            imag = jnp.sum(wr * bi - wi * br, axis=0, keepdims=True)
            mixed_ref[pl.ds(ci * 8 + mode, 1), lanes] = real
            mixed_ref[pl.ds(ci * 8 + mode + 4, 1), lanes] = imag
    copies += to_plane_cells(mixed_ref[...], high_ref, low_ref, cells_ref, out_ref, out_hbm, sems)
    for copy in copies:
        copy.wait()


def gradient_kernel(forward_ref, backward_ref, out_ref, flat_ref, wide_ref):
    part = pl.program_id(0)
    flat_ref[...] = backward_ref[...].reshape(C * 8, 128)

    for mode in range(4):
        br = flat_ref[pl.ds(mode, C, stride=8), :]
        bi = flat_ref[pl.ds(mode + 4, C, stride=8), :]
        first = jnp.where(part == 0, br, bi)
        second = jnp.where(part == 0, bi, -br)
        for ci in range(C):
            sr = forward_ref[ci, pl.ds(mode, 1), :]
            si = forward_ref[ci, pl.ds(mode + 4, 1), :]
            value = first * sr + second * si
            value = jnp.concatenate([value, jnp.zeros((128 - C, 128), f32)])
            wide_ref[pl.ds(ci * 4 + mode, 128, stride=PAIRS), :] = value.T
    out_ref[0, 0] = wide_ref[:, pl.ds(0, C)]


def activation(hidden):
    cumulative = 0.5 * (1.0 + lax.erf(hidden * half_root))
    slopes = cumulative + hidden * density_norm * jnp.exp(-0.5 * hidden * hidden)
    return (hidden * cumulative, slopes)


def pointwise_kernel(dims, weight_ref, bias_ref, cells_ref, out_ref):
    rows = C * 32
    owner = lax.broadcasted_iota(jnp.int32, (rows, C), 0) // 32
    slot = lax.broadcasted_iota(jnp.int32, (rows, C), 1)
    chooser = (owner == slot).astype(f32).astype(bf16)
    row = lax.broadcasted_iota(jnp.int32, (rows, rows), 0)
    column = lax.broadcasted_iota(jnp.int32, (rows, rows), 1)
    tall = dot(chooser, weight_ref[...], dims).astype(bf16)
    wide = dot(tall, chooser, NT_DIMS)
    mix = jnp.where(row % 32 == column % 32, wide, 0.0).astype(bf16)
    kept = jnp.where(owner == slot, jnp.broadcast_to(bias_ref[...], (rows, C)), 0.0)
    bias = jnp.sum(kept, axis=1, keepdims=True)
    for s in range(ZT // BLOCK):
        lanes = pl.ds(s * BLOCK, BLOCK)
        out_ref[:, lanes] = dot(mix, cells_ref[:, lanes], NN) + bias


def layer_kernel(
    recv_ref, table_ref, local_hbm, cotangent_hbm,
    out_hbm, gradient_hbm, sent_hbm,
    local_ref, cotangent_ref, out_ref, gradient_ref, sent_ref, sems,
):
    blocks = ZT // BLOCK
    columns = [pl.ds(s * BLOCK, BLOCK) for s in range(blocks)]
    local_copies = []
    cotangent_copies = []
    for s, lanes in enumerate(columns):
        local_copies.append(start(local_hbm.at[:, lanes], local_ref.at[:, lanes], sems.at[2 + s]))
        cotangent_copies.append(
            start(cotangent_hbm.at[:, lanes], cotangent_ref.at[:, lanes], sems.at[6 + s])
        )
    high, low = split(recv_ref[...].T)
    total = None
    copies = []
    for s, lanes in enumerate(columns):
        table = table_ref[:, lanes]
        spectral = dot(high, table, NN) + dot(low, table, NN)
        local_copies[s].wait()
        activated, slopes = activation(spectral + local_ref[:, lanes])
        out_ref[:, lanes] = activated.astype(bf16)
        copies.append(start(out_ref.at[:, lanes], out_hbm.at[:, lanes], sems.at[10 + s]))
        cotangent_copies[s].wait()
        gradient = (cotangent_ref[:, lanes].astype(f32) * slopes).astype(bf16)
        gradient_ref[:, lanes] = gradient
        copies.append(start(gradient_ref.at[:, lanes], gradient_hbm.at[:, lanes], sems.at[14 + s]))
        partial = dot(table, gradient, NT_DIMS)
        total = partial if total is None else total + partial
    sent_ref[...] = total.reshape(sent_ref.shape)
    copies.append(start(sent_ref, sent_hbm, sems.at[18]))
    for copy in copies:
        copy.wait()


def sums_kernel(cells_ref, gradient_ref, out_ref):
    rows = C * 32
    gram = dot(cells_ref[...], gradient_ref[...], NT_DIMS)
    row = lax.broadcasted_iota(jnp.int32, (rows, rows), 0)
    column = lax.broadcasted_iota(jnp.int32, (rows, rows), 1)
    kept = jnp.where(row % 32 == column % 32, gram, 0.0)
    folded = jnp.sum(kept.reshape(C, 32, rows), axis=1)
    ones = jnp.ones((8, ZT), bf16)
    bias = dot(ones, gradient_ref[...], NT_DIMS)
    values = jnp.concatenate([folded, bias[:4]], axis=0)
    owner = lax.broadcasted_iota(jnp.int32, (rows, 32), 0) // 32
    slot = lax.broadcasted_iota(jnp.int32, (rows, 32), 1)
    chooser = (owner == slot).astype(f32)
    small = lax.dot_general(
        values, chooser, (NN, ((), ())), precision=highest, preferred_element_type=f32
    )
    out_ref[...] = jnp.concatenate(
        [small[0:8], small[8:16], small[16:24], jnp.zeros((8, 32), f32)], axis=1
    )


def final_kernel(
    scaling, recv_ref, table_ref, local_hbm, out_hbm, weight_ref, bias_ref,
    local_ref, out_ref, sems,
):
    blocks = ZT // BLOCK
    columns = [pl.ds(s * BLOCK, BLOCK) for s in range(blocks)]
    local_copies = [
        start(local_hbm.at[:, lanes], local_ref.at[:, lanes], sems.at[2 + s])
        for s, lanes in enumerate(columns)
    ]
    devices = recv_ref.shape[0]
    values = recv_ref[:, :, pl.ds(0, C * 32)].reshape(devices * 8, C * 32)
    high, low = split(values.T)
    copies = []
    for s, lanes in enumerate(columns):
        table = table_ref[:, lanes]
        spectral = dot(high, table, NN) + dot(low, table, NN)
        local_copies[s].wait()
        out_ref[:, lanes] = (spectral + local_ref[:, lanes]).astype(bf16)
        copies.append(start(out_ref.at[:, lanes], out_hbm.at[:, lanes], sems.at[6 + s]))
    sums = jnp.sum(recv_ref[:, :, pl.ds(C * 32, 128)], axis=0) * scaling
    weight_ref[pl.ds(0, 8), :] = sums[:, 0:C]
    weight_ref[pl.ds(8, 8), :] = sums[:, 32 : 32 + C]
    weight_ref[pl.ds(16, 4), :] = sums[:4, 64 : 64 + C]
    bias_ref[...] = sums[4:5, 64 : 64 + C]
    for copy in copies:
        copy.wait()


def plane_kernel(first_local, second_local, first_groups, second_groups, high_out, low_out, part_ref):
    nx = first_local * first_groups
    ny = second_local * second_groups
    cells = nx * ny
    local = first_local * second_local
    cell = lax.broadcasted_iota(jnp.int32, (16, cells), 1)
    mode = lax.broadcasted_iota(jnp.int32, (16, cells), 0)
    group = cell // local
    x = (group // second_groups) * first_local + (cell % local) // second_local
    y = (group % second_groups) * second_local + cell % second_local

    def waves(length, count, position):
        frequency = jnp.where(mode < count // 2, mode, mode + length - count)
        phase = (frequency * position) % length
        phase = jnp.where(phase >= length // 2, phase - length, phase)
        angle = phase.astype(f32) * (2.0 * math.pi / length)
        return jnp.cos(angle) / math.sqrt(length), jnp.sin(angle) / math.sqrt(length)

    for slot, values in enumerate((*waves(nx, MX, x), *waves(ny, MY, y))):
        part_ref[slot] = values
    cy = part_ref[2]
    sy = part_ref[3]
    for kx in range(MX):
        cx = part_ref[0, pl.ds(kx, 1), :]
        sx = part_ref[1, pl.ds(kx, 1), :]
        for offset, values in ((0, cx * cy - sx * sy), (AB, sx * cy + cx * sy)):
            high, low = split(values)
            place = pl.ds(offset + kx * MY, MY)
            high_out[place, :] = high
            low_out[place, :] = low


def exchange(values):
    return lax.all_to_all(values, ("gx", "gy"), split_axis=0, concat_axis=0, tiled=True)


def cost(flops, nbytes):
    return pl.CostEstimate(flops=int(flops), bytes_accessed=int(nbytes), transcendentals=0)


def fast_on_device(features, spectral_weight, pointwise_weight, pointwise_bias, cotangent):
    first_local = features.shape[1]
    second_local = features.shape[2]
    first_groups = lax.axis_size("gx")
    second_groups = lax.axis_size("gy")
    devices = first_groups * second_groups
    local = first_local * second_local
    rows = C * local
    cells = devices * local
    quads = devices // 4
    depth = jnp.asarray(depth_rows(devices).astype(jnp.bfloat16))
    flat = from_hbm(features.reshape(rows, ZT))
    hbm = whole(pltpu.HBM)
    near = whole()

    sent = pl.pallas_call(
        depth_kernel,
        out_shape=in_hbm((devices, 8, rows), f32),
        in_specs=[hbm, hbm],
        out_specs=hbm,
        scratch_shapes=[
            pltpu.VMEM((2 * MZT, ZT), bf16),
            pltpu.VMEM((rows, ZT), bf16),
            pltpu.VMEM((devices, 8, rows), f32),
            pltpu.SemaphoreType.DMA((1 + 2 * (rows // 128),)),
        ],
        compiler_params=compiler(8),
        name="depth",
    )(from_hbm(depth), flat)
    received = exchange(sent)

    stored = spectral_weight.transpose(0, 1, 2, 3, 5, 4).reshape(2, 2, 128 * PAIRS, C)
    weight = pl.pallas_call(
        weight_kernel,
        out_shape=in_hbm((2, 4, 2, C, CP, 128), f32),
        grid=(2, 2),
        in_specs=[pl.BlockSpec((1, 1, 128 * PAIRS, C), lambda k, h: (k, h, 0, 0))],
        out_specs=pl.BlockSpec((1, 4, 1, C, CP, 128), lambda k, h: (h, 0, k, 0, 0, 0)),
        scratch_shapes=[pltpu.VMEM((128 * PAIRS, 128), f32)],
        compiler_params=compiler(22),
        cost_estimate=cost(1e6, 25e6),
        name="weights",
    )(from_hbm(stored))
    high, low = pl.pallas_call(
        functools.partial(plane_kernel, first_local, second_local, first_groups, second_groups),
        out_shape=(jax.ShapeDtypeStruct((2 * AB, cells), bf16),) * 2,
        in_specs=[],
        out_specs=[near] * 2,
        scratch_shapes=[pltpu.VMEM((4, 16, cells), f32)],
        compiler_params=compiler(6),
        cost_estimate=cost(1e8, 2e6),
        name="planes",
    )()

    def pointwise(dims, bias, values, name):
        return pl.pallas_call(
            functools.partial(pointwise_kernel, dims),
            out_shape=in_hbm((rows, ZT), f32),
            in_specs=[near] * 3,
            out_specs=near,
            compiler_params=compiler(12),
            cost_estimate=cost(1e9, 5e6),
            name=name,
        )(pointwise_weight, bias, values)

    plane_scratch = [
        pltpu.VMEM((2, 4, 2, C, CP, 128), f32),
        pltpu.VMEM((C, 8, AB), f32),
        pltpu.VMEM((C * 8, cells), f32),
    ]
    back_out, modes = pl.pallas_call(
        forward_kernel,
        out_shape=(in_hbm((quads, 4, 8, rows), f32), in_hbm((C, 8, AB), f32)),
        in_specs=[near, near, near, hbm],
        out_specs=(hbm, hbm),
        scratch_shapes=plane_scratch
        + [
            pltpu.VMEM((2, C * 8, 128), f32),
            pltpu.VMEM((quads, 4, 8, rows), f32),
            pltpu.SemaphoreType.DMA((21,)),
        ],
        compiler_params=compiler(20),
        name="forward_modes",
    )(received.reshape(quads, 4, 8, rows), high, low, from_hbm(weight))
    returned = exchange(back_out.reshape(devices, 8, rows)).reshape(2 * MZT, rows)

    local_ahead = pointwise(NT_DIMS, pointwise_bias.reshape(1, C), flat, "pointwise_ahead")
    layer_output, hidden_gradient, sent_back = pl.pallas_call(
        layer_kernel,
        out_shape=(
            in_hbm((rows, ZT), bf16),
            in_hbm((rows, ZT), bf16),
            in_hbm((devices, 8, rows), f32),
        ),
        in_specs=[near, near, hbm, hbm],
        out_specs=(hbm, hbm, hbm),
        scratch_shapes=[
            pltpu.VMEM((rows, ZT), f32),
            pltpu.VMEM((rows, ZT), bf16),
            pltpu.VMEM((rows, ZT), bf16),
            pltpu.VMEM((rows, ZT), bf16),
            pltpu.VMEM((devices, 8, rows), f32),
            pltpu.SemaphoreType.DMA((19,)),
        ],
        compiler_params=compiler(24),
        name="layer",
    )(returned, depth, from_hbm(local_ahead), from_hbm(cotangent.reshape(rows, ZT)))
    received_back = exchange(sent_back)

    sums = pl.pallas_call(
        sums_kernel,
        out_shape=jax.ShapeDtypeStruct((8, 128), f32),
        in_specs=[near] * 2,
        out_specs=near,
        compiler_params=compiler(12),
        cost_estimate=cost(1e9, 3e6),
        name="sums",
    )(flat, from_hbm(hidden_gradient))

    local_back = pointwise(NN, jnp.zeros((1, C), f32), from_hbm(hidden_gradient), "pointwise_back")
    wide = rows + 128
    back_cells, back_modes = pl.pallas_call(
        backward_kernel,
        out_shape=(in_hbm((quads, 4, 8, wide), f32), in_hbm((C, 8, AB), f32)),
        in_specs=[near, near, near, hbm, near],
        out_specs=(hbm, hbm),
        scratch_shapes=plane_scratch
        + [
            pltpu.VMEM((2, CP * 8, 128), f32),
            pltpu.VMEM((C * 8, AB), f32),
            pltpu.VMEM((quads, 4, 8, wide), f32),
            pltpu.SemaphoreType.DMA((21,)),
        ],
        compiler_params=compiler(20),
        name="backward_modes",
    )(received_back.reshape(quads, 4, 8, rows), high, low, from_hbm(weight), sums)
    returned_back = exchange(back_cells.reshape(devices, 8, wide))

    gradient = pl.pallas_call(
        gradient_kernel,
        out_shape=in_hbm((2, 2, 128 * PAIRS, C), f32),
        grid=(2, 2),
        in_specs=[
            pl.BlockSpec((C, 8, 128), lambda k, h: (0, 0, h)),
            pl.BlockSpec((C, 8, 128), lambda k, h: (0, 0, h)),
        ],
        out_specs=pl.BlockSpec((1, 1, 128 * PAIRS, C), lambda k, h: (k, h, 0, 0)),
        scratch_shapes=[pltpu.VMEM((C * 8, 128), f32), pltpu.VMEM((128 * PAIRS, 128), f32)],
        compiler_params=compiler(20),
        cost_estimate=cost(1e6, 25e6),
        name="spectral_gradient",
    )(modes, back_modes)
    spectral_gradient = gradient.reshape(2, MX, MY, C, 4, C).transpose(0, 1, 2, 3, 5, 4)

    features_gradient, pointwise_gradient, bias_gradient = pl.pallas_call(
        functools.partial(final_kernel, 1.0 / math.sqrt(cells * ZT)),
        out_shape=(
            in_hbm((rows, ZT), bf16),
            jax.ShapeDtypeStruct((C, C), f32),
            jax.ShapeDtypeStruct((1, C), f32),
        ),
        in_specs=[near, near, hbm],
        out_specs=(hbm, near, near),
        scratch_shapes=[
            pltpu.VMEM((rows, ZT), f32),
            pltpu.VMEM((rows, ZT), bf16),
            pltpu.SemaphoreType.DMA((10,)),
        ],
        compiler_params=compiler(16),
        name="features_gradient",
    )(returned_back, depth, from_hbm(local_back))

    return (
        layer_output.reshape(features.shape),
        features_gradient.reshape(features.shape),
        spectral_gradient,
        pointwise_gradient,
        bias_gradient.reshape(C),
    )


def kept_frequencies(length, mode_count):
    column = jnp.arange(mode_count, dtype=jnp.int32)
    return jnp.where(column < mode_count // 2, column, length - mode_count + column)


def complex_table(length, mode_count):
    phases = (
        kept_frequencies(length, mode_count)[:, None]
        * jnp.arange(length, dtype=jnp.int32)[None, :]
        % length
    )
    angles = 2.0 * math.pi / length * phases.astype(jnp.float32)
    scaling = 1.0 / math.sqrt(length)
    cosine_part = jnp.cos(angles) * scaling
    sine_part = -jnp.sin(angles) * scaling
    return jnp.stack([jnp.stack([cosine_part, -sine_part]), jnp.stack([sine_part, cosine_part])])


def make_depth_table():
    depth_phase = jnp.arange(NZ, dtype=jnp.int32)[:, None] * kept_frequencies(NZ, MZ)[None, :] % NZ
    time_phase = jnp.arange(NT, dtype=jnp.int32)[:, None] * kept_frequencies(NT, MT)[None, :] % NT
    phases = (depth_phase[:, None, :, None] * NT + time_phase[None, :, None, :] * NZ) % (NZ * NT)
    angles = 2.0 * math.pi / (NZ * NT) * phases.astype(jnp.float32)
    scaling = 1.0 / math.sqrt(NZ * NT)
    entries = jnp.stack([jnp.cos(angles) * scaling, -jnp.sin(angles) * scaling], axis=2)
    return entries.reshape(NZ * NT, 2, MZ * MT).astype(jnp.bfloat16)


def wide_activation(hidden):
    cumulative = 0.5 * (1.0 + lax.erf(hidden * half_root))
    slopes = cumulative + hidden * density_norm * jnp.exp(-0.5 * hidden * hidden)
    return (hidden * cumulative, slopes)


def contract(form, weight_part, value_part):
    return jnp.einsum(form, weight_part, value_part, precision=highest)


def mix_forward(weights, values):
    form = "abcdm,cabm->dabm"
    real_out = contract(form, weights[0], values[0]) - contract(form, weights[1], values[1])
    imaginary = contract(form, weights[0], values[1]) + contract(form, weights[1], values[0])
    return jnp.stack([real_out, imaginary])


def mix_adjoint(weights, values):
    form = "abcdm,dabm->cabm"
    real_out = contract(form, weights[0], values[0]) + contract(form, weights[1], values[1])
    imaginary = contract(form, weights[0], values[1]) - contract(form, weights[1], values[0])
    return jnp.stack([real_out, imaginary])


def weight_gradient(back_values, values):
    form = "dabm,cabm->abcdm"
    real_out = contract(form, back_values[0], values[0]) + contract(form, back_values[1], values[1])
    imaginary = contract(form, back_values[1], values[0]) - contract(
        form, back_values[0], values[1]
    )
    return jnp.stack([real_out, imaginary])


def on_device(features, spectral_weight, pointwise_weight, pointwise_bias, cotangent):
    first_local = features.shape[1]
    second_local = features.shape[2]
    first_groups = lax.axis_size("gx")
    second_groups = lax.axis_size("gy")
    first_table = complex_table(first_local * first_groups, MX)
    second_table = complex_table(second_local * second_groups, MY)
    depth_rounded = make_depth_table()
    depth_float = lax.optimization_barrier(depth_rounded).astype(jnp.float32)
    first_grid_table = first_table.reshape(2, 2, MX, first_groups, first_local)
    second_grid_table = second_table.reshape(2, 2, MY, second_groups, second_local)

    def to_modes(cell_data):
        flattened = cell_data.reshape(2, C, first_local * second_local, MZT)
        arrived = lax.all_to_all(flattened, ("gx", "gy"), split_axis=3, concat_axis=2, tiled=True)
        blocks_grid = arrived.reshape(
            2, C, first_groups, second_groups, first_local, second_local, arrived.shape[3]
        )
        partly = jnp.einsum(
            "okagx,kcghxym->ocahym", first_grid_table, blocks_grid, precision=highest
        )
        return jnp.einsum("okbhy,kcahym->ocabm", second_grid_table, partly, precision=highest)

    def to_cells(values):
        partly = jnp.einsum("kobhy,kcabm->ocahym", second_grid_table, values, precision=highest)
        blocks_grid = jnp.einsum(
            "koagx,kcahym->ocghxym", first_grid_table, partly, precision=highest
        )
        flattened = blocks_grid.reshape(
            2, C, first_groups * second_groups * first_local * second_local, blocks_grid.shape[6]
        )
        returned = lax.all_to_all(flattened, ("gx", "gy"), split_axis=2, concat_axis=3, tiled=True)
        return returned.reshape(2, C, first_local, second_local, MZT)

    spectrum_cells = jnp.einsum(
        "cxys,skm->kcxym", features, depth_rounded, preferred_element_type=jnp.float32
    )
    spectrum = to_modes(spectrum_cells)
    mixed_modes = mix_forward(spectral_weight, spectrum)
    spectral = jnp.einsum("kcxym,skm->cxys", to_cells(mixed_modes), depth_float, precision=highest)
    pointwise = jnp.einsum(
        "ab,axys->bxys", pointwise_weight, features, preferred_element_type=jnp.float32
    )
    hidden = spectral + pointwise + pointwise_bias[:, None, None, None]
    activated, slopes = wide_activation(hidden)
    layer_output = activated.astype(jnp.bfloat16)
    hidden_gradient = (cotangent.astype(jnp.float32) * slopes).astype(jnp.bfloat16)
    weight_terms = jnp.einsum(
        "axys,bxys->ab", features, hidden_gradient, preferred_element_type=jnp.float32
    )
    bias_terms = jnp.sum(hidden_gradient, axis=(1, 2, 3), dtype=jnp.float32)
    weight_total, bias_total = lax.psum((weight_terms, bias_terms), ("gx", "gy"))
    back_input = jnp.einsum(
        "cxys,skm->kcxym", hidden_gradient, depth_rounded, preferred_element_type=jnp.float32
    )
    back_spectrum = to_modes(back_input)
    spectral_gradient = weight_gradient(back_spectrum, spectrum)
    back_mixed = mix_adjoint(spectral_weight, back_spectrum)
    back_cells = jnp.einsum("kcxym,skm->cxys", to_cells(back_mixed), depth_float, precision=highest)
    back_pointwise = jnp.einsum(
        "ab,bxys->axys", pointwise_weight, hidden_gradient, preferred_element_type=jnp.float32
    )
    features_gradient = (back_cells + back_pointwise).astype(jnp.bfloat16)
    total_cells = first_local * first_groups * second_local * second_groups * NZ * NT
    scaling = 1.0 / math.sqrt(total_cells)
    return (
        layer_output,
        features_gradient,
        spectral_gradient,
        weight_total * scaling,
        bias_total * scaling,
    )


def place(features, spectral_weight, pointwise_weight, pointwise_bias, cotangent):
    fits = (
        spectral_weight.shape[5] == 4
        and features.shape[1] * features.shape[2] == 32
        and features.shape[3] == ZT
    )
    run = fast_on_device if fits else on_device
    return run(features, spectral_weight, pointwise_weight, pointwise_bias, cotangent)


def solution(mesh):
    return jax.shard_map(
        place,
        mesh=mesh,
        in_specs=(
            P(None, "gx", "gy", None),
            P(None, None, None, None, None, ("gx", "gy")),
            P(),
            P(),
            P(None, "gx", "gy", None),
        ),
        out_specs=(
            P(None, "gx", "gy", None),
            P(None, "gx", "gy", None),
            P(None, None, None, None, None, ("gx", "gy")),
            P(),
            P(),
        ),
        check_vma=False,
    )
```

```python
import functools
import math

import jax
import jax.numpy as jnp
import numpy as np
from jax import lax
from jax.experimental import pallas as pl
from jax.experimental.pallas import tpu as pltpu
from jax.sharding import PartitionSpec as P

C = 20
MX = 16
MY = 16
MZ = 16
MT = 8
NZ = 64
NT = 16
MZT = 128
ZT = NZ * NT
AB = MX * MY
CP = 24
PAIRS = C * 4
BLOCK = 256


half_root = 0.7071067811865476
density_norm = 0.3989422804014327
highest = lax.Precision.HIGHEST
f32 = jnp.float32
bf16 = jnp.bfloat16


def frequencies(length, mode_count):
    column = np.arange(mode_count)
    return np.where(column < mode_count // 2, column, length - mode_count + column)


def depth_rows(devices):
    kz = frequencies(NZ, MZ)
    kt = frequencies(NT, MT)
    z = np.arange(NZ)
    t = np.arange(NT)
    phase = (
        (kz[:, None, None, None] * z[None, None, :, None] * NT)
        + (kt[None, :, None, None] * t[None, None, None, :] * NZ)
    ) % ZT
    angle = 2.0 * np.pi / ZT * phase.reshape(MZT, ZT)
    parts = np.stack([np.cos(angle), -np.sin(angle)]) / math.sqrt(ZT)
    local = MZT // devices
    rows = parts.reshape(2, devices, local, ZT).transpose(1, 0, 2, 3)
    return rows.reshape(2 * MZT, ZT).astype(np.float32)


def split(values):
    high = values.astype(bf16)
    return high, (values - high.astype(f32)).astype(bf16)


def dot(left, right, dims):
    return lax.dot_general(left, right, (dims, ((), ())), preferred_element_type=f32)


NN = ((1,), (0,))
NT_DIMS = ((1,), (1,))


def start(source, target, sem):
    copy = pltpu.make_async_copy(source, target, sem)
    copy.start()
    return copy


def compiler(mebibytes):
    return pltpu.CompilerParams(vmem_limit_bytes=mebibytes * 1024 * 1024)


def whole(memory=pltpu.VMEM):
    return pl.BlockSpec(memory_space=memory)


def in_hbm(shape, dtype):
    return pltpu.HBM(shape, dtype)


def from_hbm(values):
    return pltpu.with_memory_space_constraint(values, pltpu.HBM)


def depth_kernel(table_hbm, cells_hbm, out_hbm, table_ref, cells_ref, out_ref, sems):
    table_copy = start(table_hbm, table_ref, sems.at[0])
    groups = cells_ref.shape[0] // 128
    blocks = [pl.ds(g * 128, 128) for g in range(groups)]
    arriving = [
        start(cells_hbm.at[block], cells_ref.at[block], sems.at[1 + g])
        for g, block in enumerate(blocks)
    ]
    table_copy.wait()
    leaving = []
    for g, block in enumerate(blocks):
        arriving[g].wait()
        out = dot(table_ref[...], cells_ref[block, :], NT_DIMS)
        out_ref[:, :, block] = out.reshape(out_ref.shape[0], 8, 128)
        leaving.append(
            start(out_ref.at[:, :, block], out_hbm.at[:, :, block], sems.at[1 + groups + g])
        )
    for copy in leaving:
        copy.wait()


def swap_blocks(tiles):
    lane = lax.broadcasted_iota(jnp.int32, tiles[0].shape, tiles[0].ndim - 1)
    axis = tiles[0].ndim - 1
    low = lane < 64
    even = (lane // 32) % 2 == 0
    t0, t1, t2, t3 = tiles

    def far(u, v):
        return jnp.where(low, u, pltpu.roll(v, 64, axis)), jnp.where(low, pltpu.roll(u, 64, axis), v)

    def near(u, v):
        return jnp.where(even, u, pltpu.roll(v, 32, axis)), jnp.where(even, pltpu.roll(u, 96, axis), v)

    a0, a2 = far(t0, t2)
    a1, a3 = far(t1, t3)
    b0, b1 = near(a0, a1)
    b2, b3 = near(a2, a3)
    return b0, b1, b2, b3


def row_sign(shape, top):
    row = lax.broadcasted_iota(jnp.int32, shape, len(shape) - 2)
    return jnp.where(row % 8 < 4, top, -top).astype(f32)


def to_plane_modes(recv_ref, high_ref, low_ref, cells_ref, modes_ref):
    for group in range(C // 4):
        lanes = pl.ds(group * 128, 128)
        tiles = [recv_ref[:, j, :, lanes] for j in range(4)]
        for i, tile in enumerate(swap_blocks(tiles)):
            for s in range(tile.shape[0]):
                cells_ref[pl.ds((group * 4 + i) * 8, 8), pl.ds(s * 128, 128)] = tile[s]
    high, low = split(cells_ref[...])
    out = (
        dot(high, high_ref[...], NT_DIMS)
        + dot(high, low_ref[...], NT_DIMS)
        + dot(low, high_ref[...], NT_DIMS)
    )
    cosine = out[:, :AB].reshape(C, 8, AB)
    sine = out[:, AB:].reshape(C, 8, AB)
    modes_ref[...] = cosine + row_sign(sine.shape, 1.0) * pltpu.roll(sine, 4, 1)


def to_plane_cells(mixed, high_ref, low_ref, cells_ref, out_ref, out_hbm, sems):
    high, low = split(mixed)

    def product(rows):
        return (
            dot(high, high_ref[rows, :], NN)
            + dot(high, low_ref[rows, :], NN)
            + dot(low, high_ref[rows, :], NN)
        ).reshape(C, 8, high_ref.shape[1])

    cosine = product(pl.ds(0, AB))
    sine = product(pl.ds(AB, AB))
    cells_ref[...] = (
        cosine + row_sign(sine.shape, -1.0) * pltpu.roll(sine, 4, 1)
    ).reshape(cells_ref.shape)
    groups = out_ref.shape[0]
    copies = []
    for group in range(C // 4):
        tiles = [
            jnp.stack(
                [
                    cells_ref[pl.ds((group * 4 + i) * 8, 8), pl.ds(s * 128, 128)]
                    for s in range(groups)
                ]
            )
            for i in range(4)
        ]
        lanes = pl.ds(group * 128, 128)
        for j, tile in enumerate(swap_blocks(tiles)):
            out_ref[:, j, :, lanes] = tile
        copies.append(
            start(out_ref.at[:, :, :, lanes], out_hbm.at[:, :, :, lanes], sems.at[group])
        )
    return copies


def weight_kernel(weight_ref, out_ref, wide_ref):
    wide_ref[:, pl.ds(0, C)] = weight_ref[0, 0]
    row = lax.broadcasted_iota(jnp.int32, (CP, 128), 0)

    def step(pair, carry):
        rows = wide_ref[pl.ds(pair, 128, stride=PAIRS), :]
        out_ref[0, pair % 4, 0, pair // 4] = jnp.where(row < C, rows.T[:CP], 0.0)
        return carry

    lax.fori_loop(0, PAIRS, step, 0, unroll=16)


def fetch_weights(weight_hbm, weight_ref, sems):
    return [
        start(
            weight_hbm.at[index // 4, index % 4], weight_ref.at[index // 4, index % 4], sems.at[13 + index]
        )
        for index in range(8)
    ]


def forward_kernel(
    recv_ref, high_ref, low_ref, weight_hbm, out_hbm, modes_out,
    weight_ref, modes_ref, cells_ref, mixed_ref, out_ref, sems,
):
    weights = fetch_weights(weight_hbm, weight_ref, sems)
    to_plane_modes(recv_ref, high_ref, low_ref, cells_ref, modes_ref)
    copies = [start(modes_ref, modes_out, sems.at[11])]

    for index in range(8):
        half = index // 4
        mode = index % 4
        lanes = pl.ds(half * 128, 128)
        weights[index].wait()
        real = jnp.zeros((CP, 128), f32)
        imag = jnp.zeros((CP, 128), f32)
        for ci in range(C):
            sr = modes_ref[ci, pl.ds(mode, 1), lanes]
            si = modes_ref[ci, pl.ds(mode + 4, 1), lanes]
            wr = weight_ref[half, mode, 0, ci]
            wi = weight_ref[half, mode, 1, ci]
            real = real + (wr * sr - wi * si)
            imag = imag + (wr * si + wi * sr)
        mixed_ref[half, pl.ds(mode, C, stride=8), :] = real[:C]
        mixed_ref[half, pl.ds(mode + 4, C, stride=8), :] = imag[:C]
    mixed = jnp.concatenate([mixed_ref[0], mixed_ref[1]], axis=1)
    copies += to_plane_cells(mixed, high_ref, low_ref, cells_ref, out_ref, out_hbm, sems)
    for copy in copies:
        copy.wait()


def backward_kernel(
    recv_ref, high_ref, low_ref, weight_hbm, out_hbm, modes_out,
    weight_ref, modes_ref, cells_ref, flat_ref, mixed_ref, out_ref, sems,
):
    weights = fetch_weights(weight_hbm, weight_ref, sems)
    to_plane_modes(recv_ref, high_ref, low_ref, cells_ref, modes_ref)
    copies = [start(modes_ref, modes_out, sems.at[11])]
    for half in range(2):
        flat_ref[half, pl.ds(0, C * 8), :] = modes_ref[:, :, pl.ds(half * 128, 128)].reshape(C * 8, 128)
        flat_ref[half, pl.ds(C * 8, (CP - C) * 8), :] = jnp.zeros(((CP - C) * 8, 128), f32)

    for index in range(8):
        half = index // 4
        mode = index % 4
        lanes = pl.ds(half * 128, 128)
        weights[index].wait()
        br = flat_ref[half, pl.ds(mode, CP, stride=8), :]
        bi = flat_ref[half, pl.ds(mode + 4, CP, stride=8), :]
        for ci in range(C):
            wr = weight_ref[half, mode, 0, ci]
            wi = weight_ref[half, mode, 1, ci]
            real = jnp.sum(wr * br + wi * bi, axis=0, keepdims=True)
            imag = jnp.sum(wr * bi - wi * br, axis=0, keepdims=True)
            mixed_ref[pl.ds(ci * 8 + mode, 1), lanes] = real
            mixed_ref[pl.ds(ci * 8 + mode + 4, 1), lanes] = imag
    copies += to_plane_cells(mixed_ref[...], high_ref, low_ref, cells_ref, out_ref, out_hbm, sems)
    for copy in copies:
        copy.wait()


def gradient_kernel(forward_ref, backward_ref, out_ref, flat_ref, wide_ref):
    part = pl.program_id(0)
    flat_ref[...] = backward_ref[...].reshape(C * 8, 128)

    for mode in range(4):
        br = flat_ref[pl.ds(mode, C, stride=8), :]
        bi = flat_ref[pl.ds(mode + 4, C, stride=8), :]
        first = jnp.where(part == 0, br, bi)
        second = jnp.where(part == 0, bi, -br)
        for ci in range(C):
            sr = forward_ref[ci, pl.ds(mode, 1), :]
            si = forward_ref[ci, pl.ds(mode + 4, 1), :]
            value = first * sr + second * si
            value = jnp.concatenate([value, jnp.zeros((128 - C, 128), f32)])
            wide_ref[pl.ds(ci * 4 + mode, 128, stride=PAIRS), :] = value.T
    out_ref[0, 0] = wide_ref[:, pl.ds(0, C)]


def activation(hidden):
    cumulative = 0.5 * (1.0 + lax.erf(hidden * half_root))
    slopes = cumulative + hidden * density_norm * jnp.exp(-0.5 * hidden * hidden)
    return (hidden * cumulative, slopes)


def spread(weight, dims):
    rows = C * 32
    owner = lax.broadcasted_iota(jnp.int32, (rows, C), 0) // 32
    slot = lax.broadcasted_iota(jnp.int32, (rows, C), 1)
    chooser = (owner == slot).astype(f32).astype(bf16)
    row = lax.broadcasted_iota(jnp.int32, (rows, rows), 0)
    column = lax.broadcasted_iota(jnp.int32, (rows, rows), 1)
    tall = dot(chooser, weight, dims).astype(bf16)
    wide = dot(tall, chooser, NT_DIMS)
    return jnp.where(row % 32 == column % 32, wide, 0.0).astype(bf16)


def pointwise_kernel(weight_ref, bias_ref, cells_ref, out_ref):
    rows = C * 32
    owner = lax.broadcasted_iota(jnp.int32, (rows, C), 0) // 32
    slot = lax.broadcasted_iota(jnp.int32, (rows, C), 1)
    mix = spread(weight_ref[...], NT_DIMS)
    kept = jnp.where(owner == slot, jnp.broadcast_to(bias_ref[...], (rows, C)), 0.0)
    bias = jnp.sum(kept, axis=1, keepdims=True)
    for s in range(ZT // BLOCK):
        lanes = pl.ds(s * BLOCK, BLOCK)
        out_ref[:, lanes] = dot(mix, cells_ref[:, lanes], NN) + bias


def layer_kernel(
    recv_ref, table_ref, local_hbm, cotangent_hbm,
    out_hbm, gradient_hbm, sent_hbm,
    local_ref, cotangent_ref, out_ref, gradient_ref, sent_ref, sems,
):
    blocks = ZT // BLOCK
    columns = [pl.ds(s * BLOCK, BLOCK) for s in range(blocks)]
    local_copies = []
    cotangent_copies = []
    for s, lanes in enumerate(columns):
        local_copies.append(start(local_hbm.at[:, lanes], local_ref.at[:, lanes], sems.at[2 + s]))
        cotangent_copies.append(
            start(cotangent_hbm.at[:, lanes], cotangent_ref.at[:, lanes], sems.at[6 + s])
        )
    high, low = split(recv_ref[...].T)
    total = None
    copies = []
    for s, lanes in enumerate(columns):
        table = table_ref[:, lanes]
        spectral = dot(high, table, NN) + dot(low, table, NN)
        local_copies[s].wait()
        activated, slopes = activation(spectral + local_ref[:, lanes])
        out_ref[:, lanes] = activated.astype(bf16)
        copies.append(start(out_ref.at[:, lanes], out_hbm.at[:, lanes], sems.at[10 + s]))
        cotangent_copies[s].wait()
        gradient = (cotangent_ref[:, lanes].astype(f32) * slopes).astype(bf16)
        gradient_ref[:, lanes] = gradient
        copies.append(start(gradient_ref.at[:, lanes], gradient_hbm.at[:, lanes], sems.at[14 + s]))
        partial = dot(table, gradient, NT_DIMS)
        total = partial if total is None else total + partial
    sent_ref[...] = total.reshape(sent_ref.shape)
    copies.append(start(sent_ref, sent_hbm, sems.at[18]))
    for copy in copies:
        copy.wait()


def products_kernel(weight_ref, cells_hbm, gradient_hbm, out_ref, local_hbm, cells_ref, gradient_ref, local_ref, sems):
    gradient_copy = start(gradient_hbm, gradient_ref, sems.at[0])
    cells_copy = start(cells_hbm, cells_ref, sems.at[1])
    rows = C * 32
    mix = spread(weight_ref[...], NN)
    gradient_copy.wait()
    copies = []
    for s in range(ZT // BLOCK):
        lanes = pl.ds(s * BLOCK, BLOCK)
        local_ref[:, lanes] = dot(mix, gradient_ref[:, lanes], NN)
        copies.append(start(local_ref.at[:, lanes], local_hbm.at[:, lanes], sems.at[2 + s]))
    cells_copy.wait()
    gram = dot(cells_ref[...], gradient_ref[...], NT_DIMS)
    row = lax.broadcasted_iota(jnp.int32, (rows, rows), 0)
    column = lax.broadcasted_iota(jnp.int32, (rows, rows), 1)
    kept = jnp.where(row % 32 == column % 32, gram, 0.0)
    folded = jnp.sum(kept.reshape(C, 32, rows), axis=1)
    ones = jnp.ones((8, ZT), bf16)
    bias = dot(ones, gradient_ref[...], NT_DIMS)
    values = jnp.concatenate([folded, bias[:4]], axis=0)
    owner = lax.broadcasted_iota(jnp.int32, (rows, 32), 0) // 32
    slot = lax.broadcasted_iota(jnp.int32, (rows, 32), 1)
    chooser = (owner == slot).astype(f32)
    small = lax.dot_general(
        values, chooser, (NN, ((), ())), precision=highest, preferred_element_type=f32
    )
    out_ref[...] = jnp.concatenate(
        [small[0:8], small[8:16], small[16:24], jnp.zeros((8, 32), f32)], axis=1
    )
    for copy in copies:
        copy.wait()


def total_kernel(scaling, own_ref, other_ref, weight_ref, bias_ref):
    sums = (own_ref[...] + other_ref[...]) * scaling
    weight_ref[pl.ds(0, 8), :] = sums[:, 0:C]
    weight_ref[pl.ds(8, 8), :] = sums[:, 32 : 32 + C]
    weight_ref[pl.ds(16, 4), :] = sums[:4, 64 : 64 + C]
    bias_ref[...] = sums[4:5, 64 : 64 + C]


def quad_kernel(own_ref, first_ref, second_ref, third_ref, out_ref):
    out_ref[...] = (own_ref[...] + first_ref[...]) + (second_ref[...] + third_ref[...])


def final_kernel(recv_ref, table_ref, local_hbm, out_hbm, local_ref, out_ref, sems):
    blocks = ZT // BLOCK
    columns = [pl.ds(s * BLOCK, BLOCK) for s in range(blocks)]
    local_copies = [
        start(local_hbm.at[:, lanes], local_ref.at[:, lanes], sems.at[2 + s])
        for s, lanes in enumerate(columns)
    ]
    high, low = split(recv_ref[...].T)
    copies = []
    for s, lanes in enumerate(columns):
        table = table_ref[:, lanes]
        spectral = dot(high, table, NN) + dot(low, table, NN)
        local_copies[s].wait()
        out_ref[:, lanes] = (spectral + local_ref[:, lanes]).astype(bf16)
        copies.append(start(out_ref.at[:, lanes], out_hbm.at[:, lanes], sems.at[6 + s]))
    for copy in copies:
        copy.wait()


def plane_kernel(first_local, second_local, first_groups, second_groups, high_out, low_out, part_ref):
    nx = first_local * first_groups
    ny = second_local * second_groups
    cells = nx * ny
    local = first_local * second_local
    cell = lax.broadcasted_iota(jnp.int32, (16, cells), 1)
    mode = lax.broadcasted_iota(jnp.int32, (16, cells), 0)
    group = cell // local
    x = (group // second_groups) * first_local + (cell % local) // second_local
    y = (group % second_groups) * second_local + cell % second_local

    def waves(length, count, position):
        frequency = jnp.where(mode < count // 2, mode, mode + length - count)
        phase = (frequency * position) % length
        phase = jnp.where(phase >= length // 2, phase - length, phase)
        angle = phase.astype(f32) * (2.0 * math.pi / length)
        return jnp.cos(angle) / math.sqrt(length), jnp.sin(angle) / math.sqrt(length)

    for slot, values in enumerate((*waves(nx, MX, x), *waves(ny, MY, y))):
        part_ref[slot] = values
    cy = part_ref[2]
    sy = part_ref[3]
    for kx in range(MX):
        cx = part_ref[0, pl.ds(kx, 1), :]
        sx = part_ref[1, pl.ds(kx, 1), :]
        for offset, values in ((0, cx * cy - sx * sy), (AB, sx * cy + cx * sy)):
            high, low = split(values)
            place = pl.ds(offset + kx * MY, MY)
            high_out[place, :] = high
            low_out[place, :] = low


def exchange(values):
    return lax.all_to_all(values, ("gx", "gy"), split_axis=0, concat_axis=0, tiled=True)


def partner(values, bit, devices):
    return lax.ppermute(values, ("gx", "gy"), [(i, i ^ bit) for i in range(devices)])


def cost(flops, nbytes):
    return pl.CostEstimate(flops=int(flops), bytes_accessed=int(nbytes), transcendentals=0)


def fast_on_device(features, spectral_weight, pointwise_weight, pointwise_bias, cotangent):
    first_local = features.shape[1]
    second_local = features.shape[2]
    first_groups = lax.axis_size("gx")
    second_groups = lax.axis_size("gy")
    devices = first_groups * second_groups
    local = first_local * second_local
    rows = C * local
    cells = devices * local
    quads = devices // 4
    depth = jnp.asarray(depth_rows(devices).astype(jnp.bfloat16))
    flat = from_hbm(features.reshape(rows, ZT))
    hbm = whole(pltpu.HBM)
    near = whole()

    sent = pl.pallas_call(
        depth_kernel,
        out_shape=in_hbm((devices, 8, rows), f32),
        in_specs=[hbm, hbm],
        out_specs=hbm,
        scratch_shapes=[
            pltpu.VMEM((2 * MZT, ZT), bf16),
            pltpu.VMEM((rows, ZT), bf16),
            pltpu.VMEM((devices, 8, rows), f32),
            pltpu.SemaphoreType.DMA((1 + 2 * (rows // 128),)),
        ],
        compiler_params=compiler(8),
        name="depth",
    )(from_hbm(depth), flat)
    received = exchange(sent)

    stored = spectral_weight.transpose(0, 1, 2, 3, 5, 4).reshape(2, 2, 128 * PAIRS, C)
    weight = pl.pallas_call(
        weight_kernel,
        out_shape=in_hbm((2, 4, 2, C, CP, 128), f32),
        grid=(2, 2),
        in_specs=[pl.BlockSpec((1, 1, 128 * PAIRS, C), lambda k, h: (k, h, 0, 0))],
        out_specs=pl.BlockSpec((1, 4, 1, C, CP, 128), lambda k, h: (h, 0, k, 0, 0, 0)),
        scratch_shapes=[pltpu.VMEM((128 * PAIRS, 128), f32)],
        compiler_params=compiler(22),
        cost_estimate=cost(1e6, 25e6),
        name="weights",
    )(from_hbm(stored))
    high, low = pl.pallas_call(
        functools.partial(plane_kernel, first_local, second_local, first_groups, second_groups),
        out_shape=(jax.ShapeDtypeStruct((2 * AB, cells), bf16),) * 2,
        in_specs=[],
        out_specs=[near] * 2,
        scratch_shapes=[pltpu.VMEM((4, 16, cells), f32)],
        compiler_params=compiler(6),
        cost_estimate=cost(1e8, 2e6),
        name="planes",
    )()

    plane_scratch = [
        pltpu.VMEM((2, 4, 2, C, CP, 128), f32),
        pltpu.VMEM((C, 8, AB), f32),
        pltpu.VMEM((C * 8, cells), f32),
    ]
    back_out, modes = pl.pallas_call(
        forward_kernel,
        out_shape=(in_hbm((quads, 4, 8, rows), f32), in_hbm((C, 8, AB), f32)),
        in_specs=[near, near, near, hbm],
        out_specs=(hbm, hbm),
        scratch_shapes=plane_scratch
        + [
            pltpu.VMEM((2, C * 8, 128), f32),
            pltpu.VMEM((quads, 4, 8, rows), f32),
            pltpu.SemaphoreType.DMA((21,)),
        ],
        compiler_params=compiler(20),
        name="forward_modes",
    )(received.reshape(quads, 4, 8, rows), high, low, from_hbm(weight))
    returned = exchange(back_out.reshape(devices, 8, rows)).reshape(2 * MZT, rows)

    local_ahead = pl.pallas_call(
        pointwise_kernel,
        out_shape=in_hbm((rows, ZT), f32),
        in_specs=[near] * 3,
        out_specs=near,
        compiler_params=compiler(12),
        cost_estimate=cost(1e9, 5e6),
        name="pointwise_ahead",
    )(pointwise_weight, pointwise_bias.reshape(1, C), flat)
    layer_output, hidden_gradient, sent_back = pl.pallas_call(
        layer_kernel,
        out_shape=(
            in_hbm((rows, ZT), bf16),
            in_hbm((rows, ZT), bf16),
            in_hbm((devices, 8, rows), f32),
        ),
        in_specs=[near, near, hbm, hbm],
        out_specs=(hbm, hbm, hbm),
        scratch_shapes=[
            pltpu.VMEM((rows, ZT), f32),
            pltpu.VMEM((rows, ZT), bf16),
            pltpu.VMEM((rows, ZT), bf16),
            pltpu.VMEM((rows, ZT), bf16),
            pltpu.VMEM((devices, 8, rows), f32),
            pltpu.SemaphoreType.DMA((19,)),
        ],
        compiler_params=compiler(24),
        name="layer",
    )(returned, depth, from_hbm(local_ahead), from_hbm(cotangent.reshape(rows, ZT)))
    received_back = exchange(sent_back)

    sums, local_back = pl.pallas_call(
        products_kernel,
        out_shape=(jax.ShapeDtypeStruct((8, 128), f32), in_hbm((rows, ZT), f32)),
        in_specs=[near, hbm, hbm],
        out_specs=(near, hbm),
        scratch_shapes=[
            pltpu.VMEM((rows, ZT), bf16),
            pltpu.VMEM((rows, ZT), bf16),
            pltpu.VMEM((rows, ZT), f32),
            pltpu.SemaphoreType.DMA((6,)),
        ],
        compiler_params=compiler(16),
        cost_estimate=cost(2e9, 6e6),
        name="products",
    )(pointwise_weight, flat, from_hbm(hidden_gradient))

    for bits in ((1, 2, 3), (4, 8, 12)):
        parts = [partner(sums, bit, devices) for bit in bits]
        sums = pl.pallas_call(
            quad_kernel,
            out_shape=jax.ShapeDtypeStruct((8, 128), f32),
            in_specs=[near] * 4,
            out_specs=near,
            compiler_params=compiler(2),
            name="quad_sum",
        )(sums, *parts)
    other = partner(sums, 16, devices)
    pointwise_gradient, bias_gradient = pl.pallas_call(
        functools.partial(total_kernel, 1.0 / math.sqrt(cells * ZT)),
        out_shape=(jax.ShapeDtypeStruct((C, C), f32), jax.ShapeDtypeStruct((1, C), f32)),
        in_specs=[near] * 2,
        out_specs=(near, near),
        compiler_params=compiler(2),
        name="total_sum",
    )(sums, other)

    back_cells, back_modes = pl.pallas_call(
        backward_kernel,
        out_shape=(in_hbm((quads, 4, 8, rows), f32), in_hbm((C, 8, AB), f32)),
        in_specs=[near, near, near, hbm],
        out_specs=(hbm, hbm),
        scratch_shapes=plane_scratch
        + [
            pltpu.VMEM((2, CP * 8, 128), f32),
            pltpu.VMEM((C * 8, AB), f32),
            pltpu.VMEM((quads, 4, 8, rows), f32),
            pltpu.SemaphoreType.DMA((21,)),
        ],
        compiler_params=compiler(20),
        name="backward_modes",
    )(received_back.reshape(quads, 4, 8, rows), high, low, from_hbm(weight))
    returned_back = exchange(back_cells.reshape(devices, 8, rows))

    gradient = pl.pallas_call(
        gradient_kernel,
        out_shape=in_hbm((2, 2, 128 * PAIRS, C), f32),
        grid=(2, 2),
        in_specs=[
            pl.BlockSpec((C, 8, 128), lambda k, h: (0, 0, h)),
            pl.BlockSpec((C, 8, 128), lambda k, h: (0, 0, h)),
        ],
        out_specs=pl.BlockSpec((1, 1, 128 * PAIRS, C), lambda k, h: (k, h, 0, 0)),
        scratch_shapes=[pltpu.VMEM((C * 8, 128), f32), pltpu.VMEM((128 * PAIRS, 128), f32)],
        compiler_params=compiler(20),
        cost_estimate=cost(1e6, 25e6),
        name="spectral_gradient",
    )(modes, back_modes)
    spectral_gradient = gradient.reshape(2, MX, MY, C, 4, C).transpose(0, 1, 2, 3, 5, 4)

    features_gradient = pl.pallas_call(
        final_kernel,
        out_shape=in_hbm((rows, ZT), bf16),
        in_specs=[near, near, hbm],
        out_specs=hbm,
        scratch_shapes=[
            pltpu.VMEM((rows, ZT), f32),
            pltpu.VMEM((rows, ZT), bf16),
            pltpu.SemaphoreType.DMA((10,)),
        ],
        compiler_params=compiler(16),
        name="features_gradient",
    )(returned_back.reshape(2 * MZT, rows), depth, from_hbm(local_back))

    return (
        layer_output.reshape(features.shape),
        features_gradient.reshape(features.shape),
        spectral_gradient,
        pointwise_gradient,
        bias_gradient.reshape(C),
    )


def kept_frequencies(length, mode_count):
    column = jnp.arange(mode_count, dtype=jnp.int32)
    return jnp.where(column < mode_count // 2, column, length - mode_count + column)


def complex_table(length, mode_count):
    phases = (
        kept_frequencies(length, mode_count)[:, None]
        * jnp.arange(length, dtype=jnp.int32)[None, :]
        % length
    )
    angles = 2.0 * math.pi / length * phases.astype(jnp.float32)
    scaling = 1.0 / math.sqrt(length)
    cosine_part = jnp.cos(angles) * scaling
    sine_part = -jnp.sin(angles) * scaling
    return jnp.stack([jnp.stack([cosine_part, -sine_part]), jnp.stack([sine_part, cosine_part])])


def make_depth_table():
    depth_phase = jnp.arange(NZ, dtype=jnp.int32)[:, None] * kept_frequencies(NZ, MZ)[None, :] % NZ
    time_phase = jnp.arange(NT, dtype=jnp.int32)[:, None] * kept_frequencies(NT, MT)[None, :] % NT
    phases = (depth_phase[:, None, :, None] * NT + time_phase[None, :, None, :] * NZ) % (NZ * NT)
    angles = 2.0 * math.pi / (NZ * NT) * phases.astype(jnp.float32)
    scaling = 1.0 / math.sqrt(NZ * NT)
    entries = jnp.stack([jnp.cos(angles) * scaling, -jnp.sin(angles) * scaling], axis=2)
    return entries.reshape(NZ * NT, 2, MZ * MT).astype(jnp.bfloat16)


def wide_activation(hidden):
    cumulative = 0.5 * (1.0 + lax.erf(hidden * half_root))
    slopes = cumulative + hidden * density_norm * jnp.exp(-0.5 * hidden * hidden)
    return (hidden * cumulative, slopes)


def contract(form, weight_part, value_part):
    return jnp.einsum(form, weight_part, value_part, precision=highest)


def mix_forward(weights, values):
    form = "abcdm,cabm->dabm"
    real_out = contract(form, weights[0], values[0]) - contract(form, weights[1], values[1])
    imaginary = contract(form, weights[0], values[1]) + contract(form, weights[1], values[0])
    return jnp.stack([real_out, imaginary])


def mix_adjoint(weights, values):
    form = "abcdm,dabm->cabm"
    real_out = contract(form, weights[0], values[0]) + contract(form, weights[1], values[1])
    imaginary = contract(form, weights[0], values[1]) - contract(form, weights[1], values[0])
    return jnp.stack([real_out, imaginary])


def weight_gradient(back_values, values):
    form = "dabm,cabm->abcdm"
    real_out = contract(form, back_values[0], values[0]) + contract(form, back_values[1], values[1])
    imaginary = contract(form, back_values[1], values[0]) - contract(
        form, back_values[0], values[1]
    )
    return jnp.stack([real_out, imaginary])


def on_device(features, spectral_weight, pointwise_weight, pointwise_bias, cotangent):
    first_local = features.shape[1]
    second_local = features.shape[2]
    first_groups = lax.axis_size("gx")
    second_groups = lax.axis_size("gy")
    first_table = complex_table(first_local * first_groups, MX)
    second_table = complex_table(second_local * second_groups, MY)
    depth_rounded = make_depth_table()
    depth_float = lax.optimization_barrier(depth_rounded).astype(jnp.float32)
    first_grid_table = first_table.reshape(2, 2, MX, first_groups, first_local)
    second_grid_table = second_table.reshape(2, 2, MY, second_groups, second_local)

    def to_modes(cell_data):
        flattened = cell_data.reshape(2, C, first_local * second_local, MZT)
        arrived = lax.all_to_all(flattened, ("gx", "gy"), split_axis=3, concat_axis=2, tiled=True)
        blocks_grid = arrived.reshape(
            2, C, first_groups, second_groups, first_local, second_local, arrived.shape[3]
        )
        partly = jnp.einsum(
            "okagx,kcghxym->ocahym", first_grid_table, blocks_grid, precision=highest
        )
        return jnp.einsum("okbhy,kcahym->ocabm", second_grid_table, partly, precision=highest)

    def to_cells(values):
        partly = jnp.einsum("kobhy,kcabm->ocahym", second_grid_table, values, precision=highest)
        blocks_grid = jnp.einsum(
            "koagx,kcahym->ocghxym", first_grid_table, partly, precision=highest
        )
        flattened = blocks_grid.reshape(
            2, C, first_groups * second_groups * first_local * second_local, blocks_grid.shape[6]
        )
        returned = lax.all_to_all(flattened, ("gx", "gy"), split_axis=2, concat_axis=3, tiled=True)
        return returned.reshape(2, C, first_local, second_local, MZT)

    spectrum_cells = jnp.einsum(
        "cxys,skm->kcxym", features, depth_rounded, preferred_element_type=jnp.float32
    )
    spectrum = to_modes(spectrum_cells)
    mixed_modes = mix_forward(spectral_weight, spectrum)
    spectral = jnp.einsum("kcxym,skm->cxys", to_cells(mixed_modes), depth_float, precision=highest)
    pointwise = jnp.einsum(
        "ab,axys->bxys", pointwise_weight, features, preferred_element_type=jnp.float32
    )
    hidden = spectral + pointwise + pointwise_bias[:, None, None, None]
    activated, slopes = wide_activation(hidden)
    layer_output = activated.astype(jnp.bfloat16)
    hidden_gradient = (cotangent.astype(jnp.float32) * slopes).astype(jnp.bfloat16)
    weight_terms = jnp.einsum(
        "axys,bxys->ab", features, hidden_gradient, preferred_element_type=jnp.float32
    )
    bias_terms = jnp.sum(hidden_gradient, axis=(1, 2, 3), dtype=jnp.float32)
    weight_total, bias_total = lax.psum((weight_terms, bias_terms), ("gx", "gy"))
    back_input = jnp.einsum(
        "cxys,skm->kcxym", hidden_gradient, depth_rounded, preferred_element_type=jnp.float32
    )
    back_spectrum = to_modes(back_input)
    spectral_gradient = weight_gradient(back_spectrum, spectrum)
    back_mixed = mix_adjoint(spectral_weight, back_spectrum)
    back_cells = jnp.einsum("kcxym,skm->cxys", to_cells(back_mixed), depth_float, precision=highest)
    back_pointwise = jnp.einsum(
        "ab,bxys->axys", pointwise_weight, hidden_gradient, preferred_element_type=jnp.float32
    )
    features_gradient = (back_cells + back_pointwise).astype(jnp.bfloat16)
    total_cells = first_local * first_groups * second_local * second_groups * NZ * NT
    scaling = 1.0 / math.sqrt(total_cells)
    return (
        layer_output,
        features_gradient,
        spectral_gradient,
        weight_total * scaling,
        bias_total * scaling,
    )


def place(features, spectral_weight, pointwise_weight, pointwise_bias, cotangent):
    fits = (
        spectral_weight.shape[5] == 4
        and features.shape[1] * features.shape[2] == 32
        and features.shape[3] == ZT
        and lax.axis_size("gx") * lax.axis_size("gy") == 32
    )
    run = fast_on_device if fits else on_device
    return run(features, spectral_weight, pointwise_weight, pointwise_bias, cotangent)


def solution(mesh):
    return jax.shard_map(
        place,
        mesh=mesh,
        in_specs=(
            P(None, "gx", "gy", None),
            P(None, None, None, None, None, ("gx", "gy")),
            P(),
            P(),
            P(None, "gx", "gy", None),
        ),
        out_specs=(
            P(None, "gx", "gy", None),
            P(None, "gx", "gy", None),
            P(None, None, None, None, None, ("gx", "gy")),
            P(),
            P(),
        ),
        check_vma=False,
    )
```

```python
import functools
import math

import jax
import jax.numpy as jnp
import numpy as np
from jax import lax
from jax.experimental import pallas as pl
from jax.experimental.pallas import tpu as pltpu
from jax.sharding import PartitionSpec as P

C = 20
MX = 16
MY = 16
MZ = 16
MT = 8
NZ = 64
NT = 16
MZT = 128
ZT = NZ * NT
AB = MX * MY
CP = 24
PAIRS = C * 4
BLOCK = 256


half_root = 0.7071067811865476
density_norm = 0.3989422804014327
highest = lax.Precision.HIGHEST
f32 = jnp.float32
bf16 = jnp.bfloat16


def frequencies(length, mode_count):
    column = np.arange(mode_count)
    return np.where(column < mode_count // 2, column, length - mode_count + column)


def depth_rows(devices):
    kz = frequencies(NZ, MZ)
    kt = frequencies(NT, MT)
    z = np.arange(NZ)
    t = np.arange(NT)
    phase = (
        (kz[:, None, None, None] * z[None, None, :, None] * NT)
        + (kt[None, :, None, None] * t[None, None, None, :] * NZ)
    ) % ZT
    angle = 2.0 * np.pi / ZT * phase.reshape(MZT, ZT)
    parts = np.stack([np.cos(angle), -np.sin(angle)]) / math.sqrt(ZT)
    local = MZT // devices
    rows = parts.reshape(2, devices, local, ZT).transpose(1, 0, 2, 3)
    return rows.reshape(2 * MZT, ZT).astype(np.float32)


def split(values):
    high = values.astype(bf16)
    return high, (values - high.astype(f32)).astype(bf16)


def dot(left, right, dims):
    return lax.dot_general(left, right, (dims, ((), ())), preferred_element_type=f32)


NN = ((1,), (0,))
NT_DIMS = ((1,), (1,))


def start(source, target, sem):
    copy = pltpu.make_async_copy(source, target, sem)
    copy.start()
    return copy


def compiler(mebibytes):
    return pltpu.CompilerParams(vmem_limit_bytes=mebibytes * 1024 * 1024)


def whole(memory=pltpu.VMEM):
    return pl.BlockSpec(memory_space=memory)


def in_hbm(shape, dtype):
    return pltpu.HBM(shape, dtype)


def from_hbm(values):
    return pltpu.with_memory_space_constraint(values, pltpu.HBM)


def depth_kernel(table_hbm, cells_hbm, out_hbm, table_ref, cells_ref, out_ref, sems):
    table_copy = start(table_hbm, table_ref, sems.at[0])
    groups = cells_ref.shape[0] // 128
    blocks = [pl.ds(g * 128, 128) for g in range(groups)]
    arriving = [
        start(cells_hbm.at[block], cells_ref.at[block], sems.at[1 + g])
        for g, block in enumerate(blocks)
    ]
    table_copy.wait()
    leaving = []
    for g, block in enumerate(blocks):
        arriving[g].wait()
        out = dot(table_ref[...], cells_ref[block, :], NT_DIMS)
        out_ref[:, :, block] = out.reshape(out_ref.shape[0], 8, 128)
        leaving.append(
            start(out_ref.at[:, :, block], out_hbm.at[:, :, block], sems.at[1 + groups + g])
        )
    for copy in leaving:
        copy.wait()


def swap_blocks(tiles):
    lane = lax.broadcasted_iota(jnp.int32, tiles[0].shape, tiles[0].ndim - 1)
    axis = tiles[0].ndim - 1
    low = lane < 64
    even = (lane // 32) % 2 == 0
    t0, t1, t2, t3 = tiles

    def far(u, v):
        return jnp.where(low, u, pltpu.roll(v, 64, axis)), jnp.where(low, pltpu.roll(u, 64, axis), v)

    def near(u, v):
        return jnp.where(even, u, pltpu.roll(v, 32, axis)), jnp.where(even, pltpu.roll(u, 96, axis), v)

    a0, a2 = far(t0, t2)
    a1, a3 = far(t1, t3)
    b0, b1 = near(a0, a1)
    b2, b3 = near(a2, a3)
    return b0, b1, b2, b3


def row_sign(shape, top):
    row = lax.broadcasted_iota(jnp.int32, shape, len(shape) - 2)
    return jnp.where(row % 8 < 4, top, -top).astype(f32)


def to_plane_modes(recv_ref, high_ref, low_ref, cells_ref, modes_ref):
    for group in range(C // 4):
        lanes = pl.ds(group * 128, 128)
        tiles = [recv_ref[:, j, :, lanes] for j in range(4)]
        for i, tile in enumerate(swap_blocks(tiles)):
            for s in range(tile.shape[0]):
                cells_ref[pl.ds((group * 4 + i) * 8, 8), pl.ds(s * 128, 128)] = tile[s]
    high, low = split(cells_ref[...])
    out = (
        dot(high, high_ref[...], NT_DIMS)
        + dot(high, low_ref[...], NT_DIMS)
        + dot(low, high_ref[...], NT_DIMS)
    )
    cosine = out[:, :AB].reshape(C, 8, AB)
    sine = out[:, AB:].reshape(C, 8, AB)
    modes_ref[...] = cosine + row_sign(sine.shape, 1.0) * pltpu.roll(sine, 4, 1)


def to_plane_cells(mixed, high_ref, low_ref, cells_ref, out_ref, out_hbm, sems):
    high, low = split(mixed)

    def product(rows):
        return (
            dot(high, high_ref[rows, :], NN)
            + dot(high, low_ref[rows, :], NN)
            + dot(low, high_ref[rows, :], NN)
        ).reshape(C, 8, high_ref.shape[1])

    cosine = product(pl.ds(0, AB))
    sine = product(pl.ds(AB, AB))
    cells_ref[...] = (
        cosine + row_sign(sine.shape, -1.0) * pltpu.roll(sine, 4, 1)
    ).reshape(cells_ref.shape)
    groups = out_ref.shape[0]
    copies = []
    for group in range(C // 4):
        tiles = [
            jnp.stack(
                [
                    cells_ref[pl.ds((group * 4 + i) * 8, 8), pl.ds(s * 128, 128)]
                    for s in range(groups)
                ]
            )
            for i in range(4)
        ]
        lanes = pl.ds(group * 128, 128)
        for j, tile in enumerate(swap_blocks(tiles)):
            out_ref[:, j, :, lanes] = tile
        copies.append(
            start(out_ref.at[:, :, :, lanes], out_hbm.at[:, :, :, lanes], sems.at[group])
        )
    return copies


def weight_kernel(weight_ref, out_ref, wide_ref):
    wide_ref[:, pl.ds(0, C)] = weight_ref[0, 0]
    row = lax.broadcasted_iota(jnp.int32, (CP, 128), 0)

    def step(pair, carry):
        rows = wide_ref[pl.ds(pair, 128, stride=PAIRS), :]
        out_ref[0, pair % 4, 0, pair // 4] = jnp.where(row < C, rows.T[:CP], 0.0)
        return carry

    lax.fori_loop(0, PAIRS, step, 0, unroll=16)


def fetch_weights(weight_hbm, weight_ref, sems):
    return [
        start(
            weight_hbm.at[index // 4, index % 4], weight_ref.at[index // 4, index % 4], sems.at[13 + index]
        )
        for index in range(8)
    ]


def forward_kernel(
    recv_ref, high_ref, low_ref, weight_hbm, out_hbm, modes_out,
    weight_ref, modes_ref, cells_ref, mixed_ref, out_ref, sems,
):
    weights = fetch_weights(weight_hbm, weight_ref, sems)
    to_plane_modes(recv_ref, high_ref, low_ref, cells_ref, modes_ref)
    copies = [start(modes_ref, modes_out, sems.at[11])]

    for index in range(8):
        half = index // 4
        mode = index % 4
        lanes = pl.ds(half * 128, 128)
        weights[index].wait()
        real = jnp.zeros((CP, 128), f32)
        imag = jnp.zeros((CP, 128), f32)
        for ci in range(C):
            sr = modes_ref[ci, pl.ds(mode, 1), lanes]
            si = modes_ref[ci, pl.ds(mode + 4, 1), lanes]
            wr = weight_ref[half, mode, 0, ci]
            wi = weight_ref[half, mode, 1, ci]
            real = real + (wr * sr - wi * si)
            imag = imag + (wr * si + wi * sr)
        mixed_ref[half, pl.ds(mode, C, stride=8), :] = real[:C]
        mixed_ref[half, pl.ds(mode + 4, C, stride=8), :] = imag[:C]
    mixed = jnp.concatenate([mixed_ref[0], mixed_ref[1]], axis=1)
    copies += to_plane_cells(mixed, high_ref, low_ref, cells_ref, out_ref, out_hbm, sems)
    for copy in copies:
        copy.wait()


def backward_kernel(
    recv_ref, high_ref, low_ref, weight_hbm, out_hbm, modes_out,
    weight_ref, modes_ref, cells_ref, flat_ref, mixed_ref, out_ref, sems,
):
    weights = fetch_weights(weight_hbm, weight_ref, sems)
    to_plane_modes(recv_ref, high_ref, low_ref, cells_ref, modes_ref)
    copies = [start(modes_ref, modes_out, sems.at[11])]
    for half in range(2):
        flat_ref[half, pl.ds(0, C * 8), :] = modes_ref[:, :, pl.ds(half * 128, 128)].reshape(C * 8, 128)
        flat_ref[half, pl.ds(C * 8, (CP - C) * 8), :] = jnp.zeros(((CP - C) * 8, 128), f32)

    for index in range(8):
        half = index // 4
        mode = index % 4
        lanes = pl.ds(half * 128, 128)
        weights[index].wait()
        br = flat_ref[half, pl.ds(mode, CP, stride=8), :]
        bi = flat_ref[half, pl.ds(mode + 4, CP, stride=8), :]
        for ci in range(C):
            wr = weight_ref[half, mode, 0, ci]
            wi = weight_ref[half, mode, 1, ci]
            real = jnp.sum(wr * br + wi * bi, axis=0, keepdims=True)
            imag = jnp.sum(wr * bi - wi * br, axis=0, keepdims=True)
            mixed_ref[pl.ds(ci * 8 + mode, 1), lanes] = real
            mixed_ref[pl.ds(ci * 8 + mode + 4, 1), lanes] = imag
    copies += to_plane_cells(mixed_ref[...], high_ref, low_ref, cells_ref, out_ref, out_hbm, sems)
    for copy in copies:
        copy.wait()


def gradient_kernel(forward_ref, backward_ref, out_ref, flat_ref, wide_ref):
    part = pl.program_id(0)
    flat_ref[...] = backward_ref[...].reshape(C * 8, 128)

    for mode in range(4):
        br = flat_ref[pl.ds(mode, C, stride=8), :]
        bi = flat_ref[pl.ds(mode + 4, C, stride=8), :]
        first = jnp.where(part == 0, br, bi)
        second = jnp.where(part == 0, bi, -br)
        for ci in range(C):
            sr = forward_ref[ci, pl.ds(mode, 1), :]
            si = forward_ref[ci, pl.ds(mode + 4, 1), :]
            value = first * sr + second * si
            value = jnp.concatenate([value, jnp.zeros((128 - C, 128), f32)])
            wide_ref[pl.ds(ci * 4 + mode, 128, stride=PAIRS), :] = value.T
    out_ref[0, 0] = wide_ref[:, pl.ds(0, C)]


def activation(hidden):
    cumulative = 0.5 * (1.0 + lax.erf(hidden * half_root))
    slopes = cumulative + hidden * density_norm * jnp.exp(-0.5 * hidden * hidden)
    return (hidden * cumulative, slopes)


def spread(weight, dims):
    rows = C * 32
    owner = lax.broadcasted_iota(jnp.int32, (rows, C), 0) // 32
    slot = lax.broadcasted_iota(jnp.int32, (rows, C), 1)
    chooser = (owner == slot).astype(f32).astype(bf16)
    row = lax.broadcasted_iota(jnp.int32, (rows, rows), 0)
    column = lax.broadcasted_iota(jnp.int32, (rows, rows), 1)
    tall = dot(chooser, weight, dims).astype(bf16)
    wide = dot(tall, chooser, NT_DIMS)
    return jnp.where(row % 32 == column % 32, wide, 0.0).astype(bf16)


def pointwise_kernel(weight_ref, bias_ref, cells_ref, out_ref):
    rows = C * 32
    owner = lax.broadcasted_iota(jnp.int32, (rows, C), 0) // 32
    slot = lax.broadcasted_iota(jnp.int32, (rows, C), 1)
    mix = spread(weight_ref[...], NT_DIMS)
    kept = jnp.where(owner == slot, jnp.broadcast_to(bias_ref[...], (rows, C)), 0.0)
    bias = jnp.sum(kept, axis=1, keepdims=True)
    for s in range(ZT // BLOCK):
        lanes = pl.ds(s * BLOCK, BLOCK)
        out_ref[:, lanes] = dot(mix, cells_ref[:, lanes], NN) + bias


def layer_kernel(
    recv_ref, table_ref, local_hbm, cotangent_hbm,
    out_hbm, gradient_hbm, sent_hbm,
    local_ref, cotangent_ref, out_ref, gradient_ref, sent_ref, sems,
):
    blocks = ZT // BLOCK
    columns = [pl.ds(s * BLOCK, BLOCK) for s in range(blocks)]
    local_copies = []
    cotangent_copies = []
    for s, lanes in enumerate(columns):
        local_copies.append(start(local_hbm.at[:, lanes], local_ref.at[:, lanes], sems.at[2 + s]))
        cotangent_copies.append(
            start(cotangent_hbm.at[:, lanes], cotangent_ref.at[:, lanes], sems.at[6 + s])
        )
    high = recv_ref[...].astype(bf16).T
    total = None
    copies = []
    for s, lanes in enumerate(columns):
        table = table_ref[:, lanes]
        spectral = dot(high, table, NN)
        local_copies[s].wait()
        activated, slopes = activation(spectral + local_ref[:, lanes])
        out_ref[:, lanes] = activated.astype(bf16)
        copies.append(start(out_ref.at[:, lanes], out_hbm.at[:, lanes], sems.at[10 + s]))
        cotangent_copies[s].wait()
        gradient = (cotangent_ref[:, lanes].astype(f32) * slopes).astype(bf16)
        gradient_ref[:, lanes] = gradient
        copies.append(start(gradient_ref.at[:, lanes], gradient_hbm.at[:, lanes], sems.at[14 + s]))
        partial = dot(table, gradient, NT_DIMS)
        total = partial if total is None else total + partial
    sent_ref[...] = total.reshape(sent_ref.shape)
    copies.append(start(sent_ref, sent_hbm, sems.at[18]))
    for copy in copies:
        copy.wait()


def products_kernel(weight_ref, cells_hbm, gradient_hbm, out_ref, local_hbm, cells_ref, gradient_ref, local_ref, sems):
    gradient_copy = start(gradient_hbm, gradient_ref, sems.at[0])
    cells_copy = start(cells_hbm, cells_ref, sems.at[1])
    rows = C * 32
    mix = spread(weight_ref[...], NN)
    gradient_copy.wait()
    copies = []
    for s in range(ZT // BLOCK):
        lanes = pl.ds(s * BLOCK, BLOCK)
        local_ref[:, lanes] = dot(mix, gradient_ref[:, lanes], NN)
        copies.append(start(local_ref.at[:, lanes], local_hbm.at[:, lanes], sems.at[2 + s]))
    cells_copy.wait()
    gram = dot(cells_ref[...], gradient_ref[...], NT_DIMS)
    row = lax.broadcasted_iota(jnp.int32, (rows, rows), 0)
    column = lax.broadcasted_iota(jnp.int32, (rows, rows), 1)
    kept = jnp.where(row % 32 == column % 32, gram, 0.0)
    folded = jnp.sum(kept.reshape(C, 32, rows), axis=1)
    ones = jnp.ones((8, ZT), bf16)
    bias = dot(ones, gradient_ref[...], NT_DIMS)
    values = jnp.concatenate([folded, bias[:4]], axis=0)
    owner = lax.broadcasted_iota(jnp.int32, (rows, 32), 0) // 32
    slot = lax.broadcasted_iota(jnp.int32, (rows, 32), 1)
    chooser = (owner == slot).astype(f32)
    small = lax.dot_general(
        values, chooser, (NN, ((), ())), precision=highest, preferred_element_type=f32
    )
    out_ref[...] = jnp.concatenate(
        [small[0:8], small[8:16], small[16:24], jnp.zeros((8, 32), f32)], axis=1
    )
    for copy in copies:
        copy.wait()


def total_kernel(scaling, own_ref, other_ref, weight_ref, bias_ref):
    sums = (own_ref[...] + other_ref[...]) * scaling
    weight_ref[pl.ds(0, 8), :] = sums[:, 0:C]
    weight_ref[pl.ds(8, 8), :] = sums[:, 32 : 32 + C]
    weight_ref[pl.ds(16, 4), :] = sums[:4, 64 : 64 + C]
    bias_ref[...] = sums[4:5, 64 : 64 + C]


def quad_kernel(own_ref, first_ref, second_ref, third_ref, out_ref):
    out_ref[...] = (own_ref[...] + first_ref[...]) + (second_ref[...] + third_ref[...])


def final_kernel(recv_ref, table_ref, local_hbm, out_hbm, local_ref, out_ref, sems):
    blocks = ZT // BLOCK
    columns = [pl.ds(s * BLOCK, BLOCK) for s in range(blocks)]
    local_copies = [
        start(local_hbm.at[:, lanes], local_ref.at[:, lanes], sems.at[2 + s])
        for s, lanes in enumerate(columns)
    ]
    high = recv_ref[...].astype(bf16).T
    copies = []
    for s, lanes in enumerate(columns):
        table = table_ref[:, lanes]
        spectral = dot(high, table, NN)
        local_copies[s].wait()
        out_ref[:, lanes] = (spectral + local_ref[:, lanes]).astype(bf16)
        copies.append(start(out_ref.at[:, lanes], out_hbm.at[:, lanes], sems.at[6 + s]))
    for copy in copies:
        copy.wait()


def plane_kernel(first_local, second_local, first_groups, second_groups, high_out, low_out, part_ref):
    nx = first_local * first_groups
    ny = second_local * second_groups
    cells = nx * ny
    local = first_local * second_local
    cell = lax.broadcasted_iota(jnp.int32, (16, cells), 1)
    mode = lax.broadcasted_iota(jnp.int32, (16, cells), 0)
    group = cell // local
    x = (group // second_groups) * first_local + (cell % local) // second_local
    y = (group % second_groups) * second_local + cell % second_local

    def waves(length, count, position):
        frequency = jnp.where(mode < count // 2, mode, mode + length - count)
        phase = (frequency * position) % length
        phase = jnp.where(phase >= length // 2, phase - length, phase)
        angle = phase.astype(f32) * (2.0 * math.pi / length)
        return jnp.cos(angle) / math.sqrt(length), jnp.sin(angle) / math.sqrt(length)

    for slot, values in enumerate((*waves(nx, MX, x), *waves(ny, MY, y))):
        part_ref[slot] = values
    cy = part_ref[2]
    sy = part_ref[3]
    for kx in range(MX):
        cx = part_ref[0, pl.ds(kx, 1), :]
        sx = part_ref[1, pl.ds(kx, 1), :]
        for offset, values in ((0, cx * cy - sx * sy), (AB, sx * cy + cx * sy)):
            high, low = split(values)
            place = pl.ds(offset + kx * MY, MY)
            high_out[place, :] = high
            low_out[place, :] = low


def exchange(values):
    return lax.all_to_all(values, ("gx", "gy"), split_axis=0, concat_axis=0, tiled=True)


def partner(values, bit, devices):
    return lax.ppermute(values, ("gx", "gy"), [(i, i ^ bit) for i in range(devices)])


def cost(flops, nbytes):
    return pl.CostEstimate(flops=int(flops), bytes_accessed=int(nbytes), transcendentals=0)


def fast_on_device(features, spectral_weight, pointwise_weight, pointwise_bias, cotangent):
    first_local = features.shape[1]
    second_local = features.shape[2]
    first_groups = lax.axis_size("gx")
    second_groups = lax.axis_size("gy")
    devices = first_groups * second_groups
    local = first_local * second_local
    rows = C * local
    cells = devices * local
    quads = devices // 4
    depth = jnp.asarray(depth_rows(devices).astype(jnp.bfloat16))
    flat = from_hbm(features.reshape(rows, ZT))
    hbm = whole(pltpu.HBM)
    near = whole()

    sent = pl.pallas_call(
        depth_kernel,
        out_shape=in_hbm((devices, 8, rows), f32),
        in_specs=[hbm, hbm],
        out_specs=hbm,
        scratch_shapes=[
            pltpu.VMEM((2 * MZT, ZT), bf16),
            pltpu.VMEM((rows, ZT), bf16),
            pltpu.VMEM((devices, 8, rows), f32),
            pltpu.SemaphoreType.DMA((1 + 2 * (rows // 128),)),
        ],
        compiler_params=compiler(8),
        name="depth",
    )(from_hbm(depth), flat)
    received = exchange(sent)

    stored = spectral_weight.transpose(0, 1, 2, 3, 5, 4).reshape(2, 2, 128 * PAIRS, C)
    weight = pl.pallas_call(
        weight_kernel,
        out_shape=in_hbm((2, 4, 2, C, CP, 128), f32),
        grid=(2, 2),
        in_specs=[pl.BlockSpec((1, 1, 128 * PAIRS, C), lambda k, h: (k, h, 0, 0))],
        out_specs=pl.BlockSpec((1, 4, 1, C, CP, 128), lambda k, h: (h, 0, k, 0, 0, 0)),
        scratch_shapes=[pltpu.VMEM((128 * PAIRS, 128), f32)],
        compiler_params=compiler(22),
        cost_estimate=cost(1e6, 25e6),
        name="weights",
    )(from_hbm(stored))
    high, low = pl.pallas_call(
        functools.partial(plane_kernel, first_local, second_local, first_groups, second_groups),
        out_shape=(jax.ShapeDtypeStruct((2 * AB, cells), bf16),) * 2,
        in_specs=[],
        out_specs=[near] * 2,
        scratch_shapes=[pltpu.VMEM((4, 16, cells), f32)],
        compiler_params=compiler(6),
        cost_estimate=cost(1e8, 2e6),
        name="planes",
    )()

    plane_scratch = [
        pltpu.VMEM((2, 4, 2, C, CP, 128), f32),
        pltpu.VMEM((C, 8, AB), f32),
        pltpu.VMEM((C * 8, cells), f32),
    ]
    back_out, modes = pl.pallas_call(
        forward_kernel,
        out_shape=(in_hbm((quads, 4, 8, rows), f32), in_hbm((C, 8, AB), f32)),
        in_specs=[near, near, near, hbm],
        out_specs=(hbm, hbm),
        scratch_shapes=plane_scratch
        + [
            pltpu.VMEM((2, C * 8, 128), f32),
            pltpu.VMEM((quads, 4, 8, rows), f32),
            pltpu.SemaphoreType.DMA((21,)),
        ],
        compiler_params=compiler(20),
        name="forward_modes",
    )(received.reshape(quads, 4, 8, rows), high, low, from_hbm(weight))
    returned = exchange(back_out.reshape(devices, 8, rows)).reshape(2 * MZT, rows)

    local_ahead = pl.pallas_call(
        pointwise_kernel,
        out_shape=in_hbm((rows, ZT), f32),
        in_specs=[near] * 3,
        out_specs=near,
        compiler_params=compiler(12),
        cost_estimate=cost(1e9, 5e6),
        name="pointwise_ahead",
    )(pointwise_weight, pointwise_bias.reshape(1, C), flat)
    layer_output, hidden_gradient, sent_back = pl.pallas_call(
        layer_kernel,
        out_shape=(
            in_hbm((rows, ZT), bf16),
            in_hbm((rows, ZT), bf16),
            in_hbm((devices, 8, rows), f32),
        ),
        in_specs=[near, near, hbm, hbm],
        out_specs=(hbm, hbm, hbm),
        scratch_shapes=[
            pltpu.VMEM((rows, ZT), f32),
            pltpu.VMEM((rows, ZT), bf16),
            pltpu.VMEM((rows, ZT), bf16),
            pltpu.VMEM((rows, ZT), bf16),
            pltpu.VMEM((devices, 8, rows), f32),
            pltpu.SemaphoreType.DMA((19,)),
        ],
        compiler_params=compiler(24),
        name="layer",
    )(returned, depth, from_hbm(local_ahead), from_hbm(cotangent.reshape(rows, ZT)))
    received_back = exchange(sent_back)

    sums, local_back = pl.pallas_call(
        products_kernel,
        out_shape=(jax.ShapeDtypeStruct((8, 128), f32), in_hbm((rows, ZT), f32)),
        in_specs=[near, hbm, hbm],
        out_specs=(near, hbm),
        scratch_shapes=[
            pltpu.VMEM((rows, ZT), bf16),
            pltpu.VMEM((rows, ZT), bf16),
            pltpu.VMEM((rows, ZT), f32),
            pltpu.SemaphoreType.DMA((6,)),
        ],
        compiler_params=compiler(16),
        cost_estimate=cost(2e9, 6e6),
        name="products",
    )(pointwise_weight, flat, from_hbm(hidden_gradient))

    for bits in ((1, 2, 3), (4, 8, 12)):
        parts = [partner(sums, bit, devices) for bit in bits]
        sums = pl.pallas_call(
            quad_kernel,
            out_shape=jax.ShapeDtypeStruct((8, 128), f32),
            in_specs=[near] * 4,
            out_specs=near,
            compiler_params=compiler(2),
            name="quad_sum",
        )(sums, *parts)
    other = partner(sums, 16, devices)
    pointwise_gradient, bias_gradient = pl.pallas_call(
        functools.partial(total_kernel, 1.0 / math.sqrt(cells * ZT)),
        out_shape=(jax.ShapeDtypeStruct((C, C), f32), jax.ShapeDtypeStruct((1, C), f32)),
        in_specs=[near] * 2,
        out_specs=(near, near),
        compiler_params=compiler(2),
        name="total_sum",
    )(sums, other)

    back_cells, back_modes = pl.pallas_call(
        backward_kernel,
        out_shape=(in_hbm((quads, 4, 8, rows), f32), in_hbm((C, 8, AB), f32)),
        in_specs=[near, near, near, hbm],
        out_specs=(hbm, hbm),
        scratch_shapes=plane_scratch
        + [
            pltpu.VMEM((2, CP * 8, 128), f32),
            pltpu.VMEM((C * 8, AB), f32),
            pltpu.VMEM((quads, 4, 8, rows), f32),
            pltpu.SemaphoreType.DMA((21,)),
        ],
        compiler_params=compiler(20),
        name="backward_modes",
    )(received_back.reshape(quads, 4, 8, rows), high, low, from_hbm(weight))
    returned_back = exchange(back_cells.reshape(devices, 8, rows))

    gradient = pl.pallas_call(
        gradient_kernel,
        out_shape=in_hbm((2, 2, 128 * PAIRS, C), f32),
        grid=(2, 2),
        in_specs=[
            pl.BlockSpec((C, 8, 128), lambda k, h: (0, 0, h)),
            pl.BlockSpec((C, 8, 128), lambda k, h: (0, 0, h)),
        ],
        out_specs=pl.BlockSpec((1, 1, 128 * PAIRS, C), lambda k, h: (k, h, 0, 0)),
        scratch_shapes=[pltpu.VMEM((C * 8, 128), f32), pltpu.VMEM((128 * PAIRS, 128), f32)],
        compiler_params=compiler(20),
        cost_estimate=cost(1e6, 25e6),
        name="spectral_gradient",
    )(modes, back_modes)
    spectral_gradient = gradient.reshape(2, MX, MY, C, 4, C).transpose(0, 1, 2, 3, 5, 4)

    features_gradient = pl.pallas_call(
        final_kernel,
        out_shape=in_hbm((rows, ZT), bf16),
        in_specs=[near, near, hbm],
        out_specs=hbm,
        scratch_shapes=[
            pltpu.VMEM((rows, ZT), f32),
            pltpu.VMEM((rows, ZT), bf16),
            pltpu.SemaphoreType.DMA((10,)),
        ],
        compiler_params=compiler(16),
        name="features_gradient",
    )(returned_back.reshape(2 * MZT, rows), depth, from_hbm(local_back))

    return (
        layer_output.reshape(features.shape),
        features_gradient.reshape(features.shape),
        spectral_gradient,
        pointwise_gradient,
        bias_gradient.reshape(C),
    )


def kept_frequencies(length, mode_count):
    column = jnp.arange(mode_count, dtype=jnp.int32)
    return jnp.where(column < mode_count // 2, column, length - mode_count + column)


def complex_table(length, mode_count):
    phases = (
        kept_frequencies(length, mode_count)[:, None]
        * jnp.arange(length, dtype=jnp.int32)[None, :]
        % length
    )
    angles = 2.0 * math.pi / length * phases.astype(jnp.float32)
    scaling = 1.0 / math.sqrt(length)
    cosine_part = jnp.cos(angles) * scaling
    sine_part = -jnp.sin(angles) * scaling
    return jnp.stack([jnp.stack([cosine_part, -sine_part]), jnp.stack([sine_part, cosine_part])])


def make_depth_table():
    depth_phase = jnp.arange(NZ, dtype=jnp.int32)[:, None] * kept_frequencies(NZ, MZ)[None, :] % NZ
    time_phase = jnp.arange(NT, dtype=jnp.int32)[:, None] * kept_frequencies(NT, MT)[None, :] % NT
    phases = (depth_phase[:, None, :, None] * NT + time_phase[None, :, None, :] * NZ) % (NZ * NT)
    angles = 2.0 * math.pi / (NZ * NT) * phases.astype(jnp.float32)
    scaling = 1.0 / math.sqrt(NZ * NT)
    entries = jnp.stack([jnp.cos(angles) * scaling, -jnp.sin(angles) * scaling], axis=2)
    return entries.reshape(NZ * NT, 2, MZ * MT).astype(jnp.bfloat16)


def wide_activation(hidden):
    cumulative = 0.5 * (1.0 + lax.erf(hidden * half_root))
    slopes = cumulative + hidden * density_norm * jnp.exp(-0.5 * hidden * hidden)
    return (hidden * cumulative, slopes)


def contract(form, weight_part, value_part):
    return jnp.einsum(form, weight_part, value_part, precision=highest)


def mix_forward(weights, values):
    form = "abcdm,cabm->dabm"
    real_out = contract(form, weights[0], values[0]) - contract(form, weights[1], values[1])
    imaginary = contract(form, weights[0], values[1]) + contract(form, weights[1], values[0])
    return jnp.stack([real_out, imaginary])


def mix_adjoint(weights, values):
    form = "abcdm,dabm->cabm"
    real_out = contract(form, weights[0], values[0]) + contract(form, weights[1], values[1])
    imaginary = contract(form, weights[0], values[1]) - contract(form, weights[1], values[0])
    return jnp.stack([real_out, imaginary])


def weight_gradient(back_values, values):
    form = "dabm,cabm->abcdm"
    real_out = contract(form, back_values[0], values[0]) + contract(form, back_values[1], values[1])
    imaginary = contract(form, back_values[1], values[0]) - contract(
        form, back_values[0], values[1]
    )
    return jnp.stack([real_out, imaginary])


def on_device(features, spectral_weight, pointwise_weight, pointwise_bias, cotangent):
    first_local = features.shape[1]
    second_local = features.shape[2]
    first_groups = lax.axis_size("gx")
    second_groups = lax.axis_size("gy")
    first_table = complex_table(first_local * first_groups, MX)
    second_table = complex_table(second_local * second_groups, MY)
    depth_rounded = make_depth_table()
    depth_float = lax.optimization_barrier(depth_rounded).astype(jnp.float32)
    first_grid_table = first_table.reshape(2, 2, MX, first_groups, first_local)
    second_grid_table = second_table.reshape(2, 2, MY, second_groups, second_local)

    def to_modes(cell_data):
        flattened = cell_data.reshape(2, C, first_local * second_local, MZT)
        arrived = lax.all_to_all(flattened, ("gx", "gy"), split_axis=3, concat_axis=2, tiled=True)
        blocks_grid = arrived.reshape(
            2, C, first_groups, second_groups, first_local, second_local, arrived.shape[3]
        )
        partly = jnp.einsum(
            "okagx,kcghxym->ocahym", first_grid_table, blocks_grid, precision=highest
        )
        return jnp.einsum("okbhy,kcahym->ocabm", second_grid_table, partly, precision=highest)

    def to_cells(values):
        partly = jnp.einsum("kobhy,kcabm->ocahym", second_grid_table, values, precision=highest)
        blocks_grid = jnp.einsum(
            "koagx,kcahym->ocghxym", first_grid_table, partly, precision=highest
        )
        flattened = blocks_grid.reshape(
            2, C, first_groups * second_groups * first_local * second_local, blocks_grid.shape[6]
        )
        returned = lax.all_to_all(flattened, ("gx", "gy"), split_axis=2, concat_axis=3, tiled=True)
        return returned.reshape(2, C, first_local, second_local, MZT)

    spectrum_cells = jnp.einsum(
        "cxys,skm->kcxym", features, depth_rounded, preferred_element_type=jnp.float32
    )
    spectrum = to_modes(spectrum_cells)
    mixed_modes = mix_forward(spectral_weight, spectrum)
    spectral = jnp.einsum("kcxym,skm->cxys", to_cells(mixed_modes), depth_float, precision=highest)
    pointwise = jnp.einsum(
        "ab,axys->bxys", pointwise_weight, features, preferred_element_type=jnp.float32
    )
    hidden = spectral + pointwise + pointwise_bias[:, None, None, None]
    activated, slopes = wide_activation(hidden)
    layer_output = activated.astype(jnp.bfloat16)
    hidden_gradient = (cotangent.astype(jnp.float32) * slopes).astype(jnp.bfloat16)
    weight_terms = jnp.einsum(
        "axys,bxys->ab", features, hidden_gradient, preferred_element_type=jnp.float32
    )
    bias_terms = jnp.sum(hidden_gradient, axis=(1, 2, 3), dtype=jnp.float32)
    weight_total, bias_total = lax.psum((weight_terms, bias_terms), ("gx", "gy"))
    back_input = jnp.einsum(
        "cxys,skm->kcxym", hidden_gradient, depth_rounded, preferred_element_type=jnp.float32
    )
    back_spectrum = to_modes(back_input)
    spectral_gradient = weight_gradient(back_spectrum, spectrum)
    back_mixed = mix_adjoint(spectral_weight, back_spectrum)
    back_cells = jnp.einsum("kcxym,skm->cxys", to_cells(back_mixed), depth_float, precision=highest)
    back_pointwise = jnp.einsum(
        "ab,bxys->axys", pointwise_weight, hidden_gradient, preferred_element_type=jnp.float32
    )
    features_gradient = (back_cells + back_pointwise).astype(jnp.bfloat16)
    total_cells = first_local * first_groups * second_local * second_groups * NZ * NT
    scaling = 1.0 / math.sqrt(total_cells)
    return (
        layer_output,
        features_gradient,
        spectral_gradient,
        weight_total * scaling,
        bias_total * scaling,
    )


def place(features, spectral_weight, pointwise_weight, pointwise_bias, cotangent):
    fits = (
        spectral_weight.shape[5] == 4
        and features.shape[1] * features.shape[2] == 32
        and features.shape[3] == ZT
        and lax.axis_size("gx") * lax.axis_size("gy") == 32
    )
    run = fast_on_device if fits else on_device
    return run(features, spectral_weight, pointwise_weight, pointwise_bias, cotangent)


def solution(mesh):
    return jax.shard_map(
        place,
        mesh=mesh,
        in_specs=(
            P(None, "gx", "gy", None),
            P(None, None, None, None, None, ("gx", "gy")),
            P(),
            P(),
            P(None, "gx", "gy", None),
        ),
        out_specs=(
            P(None, "gx", "gy", None),
            P(None, "gx", "gy", None),
            P(None, None, None, None, None, ("gx", "gy")),
            P(),
            P(),
        ),
        check_vma=False,
    )
```
